128 devices in a mesh: geo: 8 (over x, core), dist: 16 (over z, y).
Axes of the slice: x: 4, y: 4, z: 4, core: 2. Of those that a mesh axis runs over, the one named last changes fastest.
Arguments:
- estimates: bfloat16 [6144, 7424], P(('geo', 'dist')), may hold values from -4 to 4
- factors: bfloat16 [6144, 7424], P(('geo', 'dist')), may hold values from -0.625 to 0.625
- variances: bfloat16 [6144, 116], P(('geo', 'dist')), may hold values from 0.019897461 to 0.5
- intersection_tracts: int32 [2048, 32], P('dist'), may hold values from 0 to 6143, as said below
- intersection_weights: int32 [2048, 32], P('dist'), may hold values from 1 to 256
Outputs:
- marginal: float32 [2048, 7424], P('dist')
- covariance: float32 [2048, 13456], P('dist')
The draws below stay inside these ranges and needn't reach their ends.
Inputs may be any that keep to these rules, and one draw needn't show every extreme that they name: `intersection_tracts`: each district's intersections are 32 different tracts among 64 consecutive ones, counted cyclically over the region.
All inputs are finite; a program needn't handle non-finite values.
Results may differ from the reference program's by a relative error of at most 0.0003.
Values may be sent and summed in bfloat16 or wider, within the bound.
A program may use at most 128 MiB of HBM per device.

```python
import math
import jax
import jax.numpy as jnp
from jax import lax

AGE_GROUPS = 116
RANK = 64
COLUMNS = 64
INTERSECTIONS = 32
WINDOW = 64
DIST_DEV = 128
TRACTS = 6144
DISTRICTS = 2048


def draw_intersection_tracts(key, part):
    first_key, second_key = jax.random.split(jax.random.fold_in(key, 7))
    starts = jax.random.randint(first_key, (DISTRICTS,), 0, TRACTS)
    starts = starts.at[0].set(TRACTS - 1).at[1].set(0)
    row_keys = jax.random.split(second_key, DISTRICTS)

    def inner_offsets(row_key):
        return jax.random.permutation(row_key, WINDOW - 2)[:INTERSECTIONS - 2] + 1
    inner = jax.vmap(inner_offsets)(row_keys)
    lowest = jnp.zeros((DISTRICTS, 1), jnp.int32)
    highest = jnp.full((DISTRICTS, 1), WINDOW - 1, jnp.int32)
    offsets = jnp.concatenate([lowest, highest, inner.astype(jnp.int32)], axis=1)
    return ((starts[:, None] + offsets) % TRACTS).astype(jnp.int32)


def plant(entries, own_key, smallest, largest):
    longest = entries.shape.index(max(entries.shape))
    spots = []
    for shift in (0, 1):
        where = [jax.random.randint(jax.random.fold_in(own_key, axis), (), 0, length) for axis, length in enumerate(entries.shape)]
        where[longest] = (where[longest] + shift) % entries.shape[longest]
        spots.append(tuple(where))
    return entries.at[spots[0]].set(smallest).at[spots[1]].set(largest)


def block_levels(key, dims, cuts, smallest, largest):
    gain = 1.0
    for position, parts in cuts:
        draws = jax.random.uniform(jax.random.fold_in(jax.random.fold_in(key, 6), position), (parts,), jnp.float32, smallest / len(cuts), largest / len(cuts))
        gain = gain * jnp.repeat(jnp.exp(draws), dims[position] // parts).reshape((-1,) + (1,) * (len(dims) - 1 - position))
    return gain


def gaussian(rng, dims, width, reach, cuts=(), held_as=jnp.bfloat16):
    factor_of = block_levels(rng, dims, cuts, -0.22, 0.18) if cuts else 1.0
    result = jax.random.normal(rng, dims, jnp.float32) * width * factor_of
    return jnp.minimum(jnp.maximum(result, -reach), reach).astype(held_as)


def setup_inputs(seed: int = 0) -> dict:
    splits = jax.random.split(jax.random.key(seed), 6)
    estimates = gaussian(splits[0], (TRACTS, AGE_GROUPS * COLUMNS), 0.3, 4.0, ((0, 128),))
    factors = gaussian(splits[1], (TRACTS, AGE_GROUPS * RANK), 0.04, 0.625, ((0, 128),))
    variances = jnp.clip(jnp.exp(math.log(0.5) - 3.224016 * jax.random.uniform(splits[2], (TRACTS, AGE_GROUPS), jnp.float32) ** block_levels(splits[2], (TRACTS, AGE_GROUPS), ((0, 128),), -0.2, 0.2)), 0.019897461, 0.5).astype(jnp.bfloat16)
    intersection_tracts = draw_intersection_tracts(jax.random.fold_in(splits[5], 71), 0)
    intersection_weights = plant(jax.random.randint(splits[4], (DISTRICTS, INTERSECTIONS), 1, 257), jax.random.fold_in(splits[4], 1), 1, 256).astype(jnp.int32)
    return {"estimates": estimates, "factors": factors, "variances": variances, "intersection_tracts": intersection_tracts, "intersection_weights": intersection_weights}


def district_block(estimates, factors, variances, tracts, weights):
    share = weights.astype(jnp.float32) / 256.0
    est_rows = jnp.take(estimates, tracts, axis=0).astype(jnp.float32)
    fac_rows = jnp.take(factors, tracts, axis=0).astype(jnp.float32)
    var_rows = jnp.take(variances, tracts, axis=0).astype(jnp.float32)
    marginal = jnp.einsum("bk,bkc->bc", share, est_rows, precision=lax.Precision.HIGHEST)
    loading = jnp.einsum("bk,bkc->bc", share, fac_rows, precision=lax.Precision.HIGHEST)
    noise = jnp.einsum("bk,bkc->bc", share * share, var_rows, precision=lax.Precision.HIGHEST)
    count = tracts.shape[0]
    shaped = loading.reshape(count, AGE_GROUPS, RANK)
    outer = jnp.einsum("dik,djk->dij", shaped, shaped, precision=lax.Precision.HIGHEST)
    outer = outer + noise[:, :, None] * jnp.eye(AGE_GROUPS, dtype=jnp.float32)[None, :, :]
    return marginal, outer.reshape(count, AGE_GROUPS * AGE_GROUPS)


def reference(estimates, factors, variances, intersection_tracts, intersection_weights):
    blocks = DISTRICTS // DIST_DEV
    tracts = intersection_tracts.reshape(blocks, DIST_DEV, INTERSECTIONS)
    weights = intersection_weights.reshape(blocks, DIST_DEV, INTERSECTIONS)

    def one_block(pair):
        return district_block(estimates, factors, variances, pair[0], pair[1])

    marginal, covariance = lax.map(one_block, (tracts, weights))
    return (marginal.reshape(DISTRICTS, AGE_GROUPS * COLUMNS),
            covariance.reshape(DISTRICTS, AGE_GROUPS * AGE_GROUPS))
```

```python
import jax
import jax.numpy as jnp
from jax import lax
from jax.experimental import pallas as pl
from jax.experimental.pallas import tpu as pltpu
from jax.sharding import PartitionSpec as P

MESH = pl.DeviceIdType.MESH
GEO, DIST = 8, 16
DEVICES = GEO * DIST
LANES = 128
ROWS = 48
TRACTS = ROWS * DEVICES
DB = 128
INTER = 32
TABLE_TILES = 58
HI, LO = 2 * TABLE_TILES, 2 * TABLE_TILES + 1
TILES = 2 * TABLE_TILES + 2
PER_GEO = 15
SLOTS = GEO * PER_GEO
CODE_ROWS = DB + 16
STEPS = 32000.0
AGES, RANK = 116, 64


def owner_tile(g, d):
    return g * PER_GEO + d


def has_tile(g, d):
    return jnp.logical_and(d < PER_GEO, owner_tile(g, d) < TILES)


def sums_kernel(idx, wgt, est, fac, var, out,
                pk, varp, table, weight, block, coded,
                local_sem, pk_send, pk_recv, row_send, row_recv,
                tile_send, slot_recv, right_send, left_send, core_send):
    g = lax.axis_index("geo")
    d = lax.axis_index("dist")
    me = g * DIST + d
    tau = owner_tile(g, d)
    mine = has_tile(g, d)

    packed = idx[...] * 512 + wgt[...]
    pk[d] = jnp.transpose(packed)

    def pk_copy(slot, to):
        return pltpu.make_async_remote_copy(
            src_ref=pk.at[slot], dst_ref=pk.at[slot], send_sem=pk_send.at[to],
            recv_sem=pk_recv.at[slot], device_id=(g, to), device_id_type=MESH)

    def pk_start(s, _):
        pk_copy(d, lax.rem(d + s, DIST)).start()
        return 0
    lax.fori_loop(1, DIST, pk_start, 0)

    varp[...] = jnp.zeros_like(varp)
    varp[:, 0:AGES] = var[...]

    def row_copy(ge, de, src, tile_ref_cols):
        e = ge * DIST + de
        return pltpu.make_async_remote_copy(
            src_ref=src.at[:, tile_ref_cols],
            dst_ref=table.at[pl.ds(pl.multiple_of(me * ROWS, 16), ROWS), :],
            send_sem=row_send.at[e], recv_sem=row_recv.at[me],
            device_id=(ge, de), device_id_type=MESH)

    def own_copy(src, cols):
        return pltpu.make_async_copy(
            src.at[:, cols],
            table.at[pl.ds(pl.multiple_of(me * ROWS, 16), ROWS), :], local_sem.at[0])

    def for_tile(t, action):
        @pl.when(t < TABLE_TILES)
        def _():
            action(est, pl.ds(pl.multiple_of(t * LANES, LANES), LANES))

        @pl.when(jnp.logical_and(t >= TABLE_TILES, t < HI))
        def _():
            action(fac, pl.ds(pl.multiple_of((t - TABLE_TILES) * LANES, LANES), LANES))

        @pl.when(jnp.logical_and(t >= HI, t < TILES))
        def _():
            action(varp, pl.ds(0, LANES))

    def row_start(s, _):
        e = lax.rem(me + s, DEVICES)
        ge, de = lax.div(e, DIST), lax.rem(e, DIST)

        @pl.when(de < PER_GEO)
        def _():
            for_tile(owner_tile(ge, de), lambda src, cols: row_copy(ge, de, src, cols).start())
        return 0

    @pl.when(mine)
    def _():
        for_tile(tau, lambda src, cols: own_copy(src, cols).start())
    lax.fori_loop(1, DEVICES, row_start, 0)

    lane = lax.broadcasted_iota(jnp.int32, (DB, LANES), 1)
    residue = lax.broadcasted_iota(jnp.int32, (64, DB), 0)

    def weights_of(s, _):
        dd = lax.rem(d + s, DIST)

        @pl.when(s > 0)
        def _():
            pk_copy(dd, d).wait_recv()
        entries = pk[dd]
        res = lax.shift_right_logical(entries, 9) & 63
        val = (lax.shift_right_logical(entries, 15) * 512) + (entries & 511)
        acc = jnp.zeros((64, DB), jnp.int32)
        for k in range(INTER):
            acc = jnp.where(residue == res[k:k + 1, :], val[k:k + 1, :], acc)
        both = jnp.transpose(jnp.concatenate([acc, acc], axis=0))
        w = both & 511
        square = w * w
        w = jnp.where(tau == HI, lax.shift_right_logical(square, 8),
                      jnp.where(tau == LO, square & 255, w))
        b = lax.shift_right_logical(both, 9) - jnp.where(lane >= 64, 1, 0)
        weight[dd] = (w.astype(jnp.float32) * (1.0 / 256.0)).astype(jnp.bfloat16)
        block[dd] = b.astype(jnp.float32).astype(jnp.bfloat16)
        return 0
    lax.fori_loop(0, DIST, weights_of, 0)

    @pl.when(mine)
    def _():
        def row_wait(s, _):
            e = lax.rem(me + DEVICES - s, DEVICES)
            at = table.at[pl.ds(pl.multiple_of(e * ROWS, 16), ROWS), :]
            pltpu.make_async_remote_copy(
                src_ref=at, dst_ref=at, send_sem=row_send.at[e], recv_sem=row_recv.at[e],
                device_id=(g, d), device_id_type=MESH).wait_recv()
            return 0
        for_tile(tau, lambda src, cols: own_copy(src, cols).wait())
        lax.fori_loop(1, DEVICES, row_wait, 0)

    x, c = lax.div(g, 2), lax.rem(g, 2)
    g_right = lax.rem(x + 1, 4) * 2 + c
    g_left = lax.rem(x + 3, 4) * 2 + c
    g_far = lax.rem(x + 2, 4) * 2 + c
    g_core = x * 2 + (1 - c)

    def slot_copy(slot, send_sem, to_g):
        return pltpu.make_async_remote_copy(
            src_ref=out.at[slot], dst_ref=out.at[slot], send_sem=send_sem,
            recv_sem=slot_recv.at[slot], device_id=(to_g, d), device_id_type=MESH)

    def tile_copy(dd):
        return pltpu.make_async_remote_copy(
            src_ref=coded.at[dd], dst_ref=out.at[tau], send_sem=tile_send.at[dd],
            recv_sem=slot_recv.at[tau], device_id=(g, dd), device_id_type=MESH)

    def own_tile_copy():
        return pltpu.make_async_copy(coded.at[d], out.at[tau], local_sem.at[1])

    def compute(dd):
        w = weight[dd]
        b = block[dd]
        acc = jnp.zeros((DB, LANES), jnp.float32)
        zero = jnp.zeros_like(w)
        for step in range(TRACTS // 256):
            parts = []
            for h in range(2):
                at = float(2 * (2 * step + h))
                parts.append(jnp.where(b == jnp.full_like(b, at), w, zero))
            acc = acc + jnp.dot(jnp.concatenate(parts, axis=1), table[step * 256:(step + 1) * 256, :],
                                preferred_element_type=jnp.float32)
        top = jnp.maximum(jnp.max(jnp.abs(acc), axis=0, keepdims=True), 1e-30)
        e = jnp.ceil(jnp.log2(top))
        code = jnp.round(acc * (STEPS / jnp.exp2(e)))
        coded[dd, 0:DB, :] = code.astype(jnp.int32).astype(jnp.int16)
        coded[dd, DB:CODE_ROWS, :] = jnp.broadcast_to(e, (16, LANES)).astype(jnp.int32).astype(jnp.int16)

    def slot_of(gg, s):
        dd = lax.rem(d + DIST - s, DIST)
        return dd, owner_tile(gg, dd), has_tile(gg, dd)

    def from_dist(s):
        dd, slot, there = slot_of(g, s)

        @pl.when(there)
        def _():
            @pl.when(s == 0)
            def _():
                own_tile_copy().wait()

            @pl.when(s > 0)
            def _():
                slot_copy(slot, tile_send.at[0], g_right).wait_recv()
            slot_copy(slot, right_send.at[0, dd], g_right).start()
            slot_copy(slot, left_send.at[0, dd], g_left).start()
            slot_copy(slot, core_send.at[0, dd], g_core).start()

    def from_side(gg, to_g, sems, parity, n, s):
        dd, slot, there = slot_of(gg, s)

        @pl.when(there)
        def _():
            slot_copy(slot, tile_send.at[0], g_right).wait_recv()

            @pl.when(lax.rem(dd, 2) == parity)
            def _():
                slot_copy(slot, sems.at[1, dd], to_g).start()
            slot_copy(slot, core_send.at[n, dd], g_core).start()

    def from_far(s):
        dd, slot, there = slot_of(g_far, s)

        @pl.when(there)
        def _():
            slot_copy(slot, tile_send.at[0], g_right).wait_recv()
            slot_copy(slot, core_send.at[3, dd], g_core).start()

    def at_step(t, lag, body):
        s = t - lag

        @pl.when(jnp.logical_and(s >= 0, s < DIST))
        def _():
            body(s)

    def send_step(s):
        dd = lax.rem(d + s, DIST)

        @pl.when(mine)
        def _():
            compute(dd)

            @pl.when(s > 0)
            def _():
                tile_copy(dd).start()

            @pl.when(s == 0)
            def _():
                own_tile_copy().start()

    def round_of(t, _):
        at_step(t, 0, send_step)
        at_step(t, 1, from_dist)
        at_step(t, 3, lambda s: from_side(g_left, g_right, right_send, 0, 1, s))
        at_step(t, 3, lambda s: from_side(g_right, g_left, left_send, 1, 2, s))
        at_step(t, 5, from_far)
        return 0
    lax.fori_loop(0, DIST + 5, round_of, 0)

    def from_core(s, _):
        for gg in (g, g_left, g_right, g_far):
            other = lax.div(gg, 2) * 2 + (1 - c)
            _, slot, there = slot_of(other, s)

            @pl.when(there)
            def _():
                slot_copy(slot, tile_send.at[0], g_right).wait_recv()
        return 0
    lax.fori_loop(0, DIST, from_core, 0)

    def sent(s, _):
        dd, slot, there = slot_of(g, s)

        @pl.when(jnp.logical_and(mine, s > 0))
        def _():
            tile_copy(dd).wait_send()

        @pl.when(s > 0)
        def _():
            pk_copy(d, dd).wait_send()

        @pl.when(there)
        def _():
            slot_copy(slot, right_send.at[0, dd], g_right).wait_send()
            slot_copy(slot, left_send.at[0, dd], g_left).wait_send()
            slot_copy(slot, core_send.at[0, dd], g_core).wait_send()
        for gg, to_g, sems, parity, n in ((g_left, g_right, right_send, 0, 1), (g_right, g_left, left_send, 1, 2)):
            dd, slot, there = slot_of(gg, s)

            @pl.when(there)
            def _():
                @pl.when(lax.rem(dd, 2) == parity)
                def _():
                    slot_copy(slot, sems.at[1, dd], to_g).wait_send()
                slot_copy(slot, core_send.at[n, dd], g_core).wait_send()
        dd, slot, there = slot_of(g_far, s)

        @pl.when(there)
        def _():
            slot_copy(slot, core_send.at[3, dd], g_core).wait_send()
        return 0
    lax.fori_loop(0, DIST, sent, 0)

    def rows_sent(s, _):
        e = lax.rem(me + s, DEVICES)
        ge, de = lax.div(e, DIST), lax.rem(e, DIST)

        @pl.when(has_tile(ge, de))
        def _():
            row_copy(ge, de, varp, pl.ds(0, LANES)).wait_send()
        return 0
    lax.fori_loop(1, DEVICES, rows_sent, 0)


def tile_sums(idx, wgt, est, fac, var):
    vmem = pl.BlockSpec(memory_space=pltpu.VMEM)
    hbm = pl.BlockSpec(memory_space=pl.ANY)
    dma = pltpu.SemaphoreType.DMA
    return pl.pallas_call(
        sums_kernel,
        out_shape=jax.ShapeDtypeStruct((SLOTS, CODE_ROWS, LANES), jnp.int16),
        in_specs=[vmem, vmem, hbm, hbm, vmem],
        out_specs=hbm,
        scratch_shapes=[
            pltpu.VMEM((DIST, INTER, DB), jnp.int32),
            pltpu.VMEM((ROWS, LANES), jnp.bfloat16),
            pltpu.VMEM((TRACTS, LANES), jnp.bfloat16),
            pltpu.VMEM((DIST, DB, LANES), jnp.bfloat16),
            pltpu.VMEM((DIST, DB, LANES), jnp.bfloat16),
            pltpu.VMEM((DIST, CODE_ROWS, LANES), jnp.int16),
            dma((2,)), dma((DIST,)), dma((DIST,)), dma((DEVICES,)), dma((DEVICES,)),
            dma((DIST,)), dma((SLOTS,)), dma((2, DIST)), dma((2, DIST)), dma((4, DIST)),
        ],
        compiler_params=pltpu.CompilerParams(has_side_effects=True, vmem_limit_bytes=48 * 2**20),
        name="tile_sums",
    )(idx, wgt, est, fac, var)


GROUP = 8
CROWS = 120


def blocks_kernel(slots_hbm, marg_hbm, cov_hbm, slots, loading, marg, noise, paired, outer, flat, in_sem, marg_sem, cov_sem):
    def fetch(i):
        start, size = ((TABLE_TILES, SLOTS - TABLE_TILES), (0, TABLE_TILES))[i]
        return pltpu.make_async_copy(slots_hbm.at[pl.ds(start, size)], slots.at[pl.ds(start, size)], in_sem.at[i])
    fetch(0).start()
    fetch(1).start()
    fetch(0).wait()

    def decode(slot):
        code = slots[slot, 0:DB, :].astype(jnp.int32).astype(jnp.float32)
        e = slots[slot, DB:CODE_ROWS, :].astype(jnp.int32).astype(jnp.float32)
        return code * (jnp.exp2(e[0:1, :]) * (1.0 / STEPS))

    noise[...] = decode(HI) + decode(LO) * (1.0 / 256.0)

    def load_tile(t, _):
        loading[pl.ds(pl.multiple_of(t * DB, DB), DB), :] = decode(TABLE_TILES + t)
        return 0
    lax.fori_loop(0, TABLE_TILES, load_tile, 0)

    fetch(1).wait()
    for t in range(TABLE_TILES):
        marg[:, t * LANES:(t + 1) * LANES] = decode(t)
    out_marg = pltpu.make_async_copy(marg, marg_hbm, marg_sem)
    out_marg.start()

    paired[...] = jnp.zeros_like(paired)
    lane_row = lax.broadcasted_iota(jnp.int32, (TABLE_TILES, LANES), 1)
    lane_full = lax.broadcasted_iota(jnp.int32, (LANES, LANES), 1)
    lane = lax.broadcasted_iota(jnp.int32, (GROUP, LANES), 1)

    def cov_copy(grp, at):
        return pltpu.make_async_copy(flat.at[at], cov_hbm.at[pl.ds(pl.multiple_of(grp * GROUP, GROUP), GROUP), :], cov_sem.at[at])

    def group(grp, _):
        at = lax.rem(grp, 2)

        @pl.when(grp >= 2)
        def _():
            cov_copy(grp - 2, at).wait()
        for k in range(GROUP):
            rows = loading[pl.ds(grp * GROUP + k, TABLE_TILES, stride=DB), :]
            turned = pltpu.roll(rows, RANK, axis=1)
            low = lane_row < RANK
            paired[k, pl.ds(0, TABLE_TILES, stride=2), :] = jnp.where(low, rows, turned)
            paired[k, pl.ds(1, TABLE_TILES, stride=2), :] = jnp.where(low, turned, rows)
        for k in range(GROUP):
            full = paired[k]
            hi = full.astype(jnp.bfloat16)
            lo = (full - hi.astype(jnp.float32)).astype(jnp.bfloat16)
            mixed = jnp.where(lane_full < RANK, hi, lo)
            left = jnp.concatenate([mixed, mixed], axis=1)
            right = jnp.concatenate([hi, lo], axis=1)
            product = lax.dot_general(left, right, (((1,), (1,)), ((), ())), preferred_element_type=jnp.float32)
            outer[k * CROWS:(k + 1) * CROWS, :] = product[0:CROWS, :]
        extra = noise[pl.ds(pl.multiple_of(grp * GROUP, GROUP), GROUP), :]
        current = None
        for i in range(AGES):
            row = outer[pl.ds(i, GROUP, stride=CROWS), :]
            row = row + jnp.where(lane == i, extra, 0.0)
            tile, off = divmod(AGES * i, LANES)
            turned = pltpu.roll(row, off, axis=1) if off else row
            current = jnp.where(lane < off, current, turned) if off else turned
            if off + AGES >= LANES:
                flat[at, :, tile * LANES:(tile + 1) * LANES] = current
                current = turned
        done = (AGES * AGES // LANES) * LANES
        flat[at, :, done:AGES * AGES] = current[:, 0:AGES * AGES - done]
        cov_copy(grp, at).start()
        return 0
    lax.fori_loop(0, DB // GROUP, group, 0)
    cov_copy(DB // GROUP - 2, 0).wait()
    cov_copy(DB // GROUP - 1, 1).wait()
    out_marg.wait()


def blocks(slots):
    hbm = pl.BlockSpec(memory_space=pl.ANY)
    dma = pltpu.SemaphoreType.DMA
    return pl.pallas_call(
        blocks_kernel,
        out_shape=(jax.ShapeDtypeStruct((DB, TABLE_TILES * LANES), jnp.float32),
                   jax.ShapeDtypeStruct((DB, AGES * AGES), jnp.float32)),
        in_specs=[hbm],
        out_specs=(hbm, hbm),
        scratch_shapes=[
            pltpu.VMEM((SLOTS, CODE_ROWS, LANES), jnp.int16),
            pltpu.VMEM((TABLE_TILES * DB, LANES), jnp.float32),
            pltpu.VMEM((DB, TABLE_TILES * LANES), jnp.float32),
            pltpu.VMEM((DB, LANES), jnp.float32),
            pltpu.VMEM((GROUP, LANES, LANES), jnp.float32),
            pltpu.VMEM((GROUP * CROWS, LANES), jnp.float32),
            pltpu.VMEM((2, GROUP, AGES * AGES), jnp.float32),
            dma((2,)), dma(()), dma((2,)),
        ],
        compiler_params=pltpu.CompilerParams(vmem_limit_bytes=48 * 2**20),
        name="district_blocks",
    )(slots)


def shards(estimates, factors, variances, intersection_tracts, intersection_weights):
    slots = tile_sums(intersection_tracts, intersection_weights, estimates, factors, variances)
    return blocks(slots)


def solution(mesh):
    return jax.shard_map(
        shards,
        mesh=mesh,
        in_specs=(
            P(("geo", "dist"), None),
            P(("geo", "dist"), None),
            P(("geo", "dist"), None),
            P("dist", None),
            P("dist", None),
        ),
        out_specs=(P("dist", None), P("dist", None)),
        check_vma=False,
    )
```

```python
import jax
import jax.numpy as jnp
from jax import lax
from jax.experimental import pallas as pl
from jax.experimental.pallas import tpu as pltpu
from jax.sharding import PartitionSpec as P

MESH = pl.DeviceIdType.MESH
GEO, DIST = 8, 16
DEVICES = GEO * DIST
LANES = 128
ROWS = 48
TRACTS = ROWS * DEVICES
BLOCK = ROWS * DIST
DB = 128
INTER = 32
TABLE_TILES = 58
HI, LO = 2 * TABLE_TILES, 2 * TABLE_TILES + 1
PER_GEO = 15
SLOTS = GEO * PER_GEO
CODE_ROWS = DB + 8
STEPS = 32000.0
AGES, RANK = 116, 64
SIDE_LAG, FAR_LAG = 4, 8


def sums_kernel(idx, wgt, est, fac, var, out,
                pk, varp, table, weight, block, sums, coded,
                ready, own_sem, pk_send, pk_recv, row_send, row_recv,
                tile_send, slot_recv, right_send, left_send, core_send, core_recv):
    g = lax.axis_index("geo")
    d = lax.axis_index("dist")
    me = g * DIST + d
    tau = g * PER_GEO + d
    mine = d < PER_GEO
    x, c = lax.div(g, 2), lax.rem(g, 2)
    g_right = lax.rem(x + 1, 4) * 2 + c
    g_left = lax.rem(x + 3, 4) * 2 + c
    g_far = lax.rem(x + 2, 4) * 2 + c
    g_core = x * 2 + (1 - c)

    barrier = pltpu.get_barrier_semaphore()
    for s in range(1, DIST):
        pl.semaphore_signal(barrier, inc=1, device_id=(g, lax.rem(d + s, DIST)), device_id_type=MESH)
    for s in range(1, GEO):
        pl.semaphore_signal(barrier, inc=1, device_id=(lax.rem(g + s, GEO), d), device_id_type=MESH)

    pk[d] = idx[...] * 512 + wgt[...]
    varp[...] = jnp.zeros_like(varp)
    varp[:, 0:AGES] = var[...]

    my_rows = table.at[pl.ds(pl.multiple_of(me * ROWS, 16), ROWS), :]

    def row_copy(ge, de, src, cols):
        return pltpu.make_async_remote_copy(
            src_ref=src.at[:, cols], dst_ref=my_rows, send_sem=row_send.at[0],
            recv_sem=row_recv.at[g], device_id=(ge, de), device_id_type=MESH)

    def for_tile(t, action):
        @pl.when(t < TABLE_TILES)
        def _():
            action(est, pl.ds(pl.multiple_of(t * LANES, LANES), LANES))

        @pl.when(jnp.logical_and(t >= TABLE_TILES, t < HI))
        def _():
            action(fac, pl.ds(pl.multiple_of((t - TABLE_TILES) * LANES, LANES), LANES))

        @pl.when(t >= HI)
        def _():
            action(varp, pl.ds(0, LANES))

    @pl.when(mine)
    def _():
        for_tile(tau, lambda src, cols: pltpu.make_async_copy(src.at[:, cols], my_rows, row_recv.at[g]).start())

    pl.semaphore_wait(barrier, DIST - 1 + GEO - 1)
    for s in range(1, GEO):
        pl.semaphore_signal(ready, inc=1, device_id=(lax.rem(g + s, GEO), d), device_id_type=MESH)

    def pk_copy(slot, to):
        return pltpu.make_async_remote_copy(
            src_ref=pk.at[slot], dst_ref=pk.at[slot], send_sem=pk_send.at[0],
            recv_sem=pk_recv.at[0], device_id=(g, to), device_id_type=MESH)

    def pk_start(s, _):
        pk_copy(d, lax.rem(d + s, DIST)).start()
        return 0
    lax.fori_loop(1, DIST, pk_start, 0)

    def rows_to(r, ks):
        ge = lax.rem(g + r, GEO)

        def one(k, _):
            de = lax.rem(d + k, DIST)

            @pl.when(de < PER_GEO)
            def _():
                for_tile(ge * PER_GEO + de, lambda src, cols: row_copy(ge, de, src, cols).start())
            return 0
        lax.fori_loop(ks, DIST, one, 0)
        return 0
    rows_to(0, 1)
    pl.semaphore_wait(ready, GEO - 1)
    lax.fori_loop(1, GEO, lambda r, _: rows_to(r, 0), 0)

    others = pk.at[pl.ds(0, DIST - 1)]
    pltpu.make_async_copy(others, others, pk_recv.at[0]).wait()
    lane = lax.broadcasted_iota(jnp.int32, (DB, LANES), 1)
    residue = lax.broadcasted_iota(jnp.int32, (64, DB), 0)

    def weights_of(dd, _):
        entries = pk[dd]
        res = lax.shift_right_logical(entries, 9) & 63
        val = (lax.shift_right_logical(entries, 15) * 512) + (entries & 511)
        acc = jnp.zeros((64, DB), jnp.int32)
        for k in range(INTER):
            acc = jnp.where(residue == res[k:k + 1, :], val[k:k + 1, :], acc)
        both = jnp.transpose(jnp.concatenate([acc, acc], axis=0))
        w = both & 511
        square = w * w
        w = jnp.where(tau == HI, lax.shift_right_logical(square, 8),
                      jnp.where(tau == LO, square & 255, w))
        b = lax.shift_right_logical(both, 9) - jnp.where(lane >= 64, 1, 0)
        weight[dd] = (w.astype(jnp.float32) * (1.0 / 256.0)).astype(jnp.bfloat16)
        block[dd] = b.astype(jnp.float32).astype(jnp.bfloat16)
        return 0
    lax.fori_loop(0, DIST, weights_of, 0)

    many = 4

    def product(q, gb):
        w = weight[pl.ds(q * many, many)].reshape(many * DB, LANES)
        b = block[pl.ds(q * many, many)].reshape(many * DB, LANES)
        zero = jnp.zeros_like(w)
        total = None
        for step in range(BLOCK // 256):
            parts = []
            for h in range(2):
                at = (2 * (gb * (BLOCK // LANES) + 2 * step + h)).astype(jnp.float32).astype(jnp.bfloat16)
                parts.append(jnp.where(b == at, w, zero))
            rows = table[pl.ds(pl.multiple_of(gb * BLOCK + step * 256, 256), 256), :]
            part = jnp.dot(jnp.concatenate(parts, axis=1), rows, preferred_element_type=jnp.float32)
            total = part if total is None else total + part
        return total.reshape(many, DB, LANES)

    def tile_copy(dd):
        return pltpu.make_async_remote_copy(
            src_ref=coded.at[dd], dst_ref=out.at[tau], send_sem=tile_send.at[0],
            recv_sem=slot_recv.at[tau], device_id=(g, dd), device_id_type=MESH)

    def own_tile_copy():
        return pltpu.make_async_copy(coded.at[d], out.at[tau], own_sem)

    def encode(dd):
        total = sums[dd]
        top = jnp.maximum(jnp.max(jnp.abs(total), axis=0, keepdims=True), 1e-30)
        e = jnp.ceil(jnp.log2(top))
        code = jnp.round(total * (STEPS / jnp.exp2(e)))
        coded[dd, 0:DB, :] = code.astype(jnp.int32).astype(jnp.int16)
        coded[dd, DB:CODE_ROWS, :] = jnp.broadcast_to(e, (8, LANES)).astype(jnp.int32).astype(jnp.int16)

    @pl.when(mine)
    def _():
        def block_of(r, _):
            gb = lax.rem(g + GEO - r, GEO)
            rows = table.at[pl.ds(pl.multiple_of(gb * BLOCK, 256), BLOCK), :]
            pltpu.make_async_copy(rows, rows, row_recv.at[gb]).wait()

            def quarter(i, _):
                q = lax.rem(lax.div(d, many) + i, DIST // many)

                @pl.when(r == 0)
                def _():
                    sums[pl.ds(q * many, many)] = product(q, gb)

                @pl.when(r > 0)
                def _():
                    sums[pl.ds(q * many, many)] += product(q, gb)

                @pl.when(r == GEO - 1)
                def _():
                    for k in range(many):
                        dd = q * many + lax.rem(lax.rem(d, many) + k, many)
                        encode(dd)

                        @pl.when(dd != d)
                        def _():
                            tile_copy(dd).start()

                        @pl.when(dd == d)
                        def _():
                            own_tile_copy().start()
                return 0
            lax.fori_loop(0, DIST // many, quarter, 0)
            return 0
        lax.fori_loop(0, GEO, block_of, 0)

    def slot_copy(slot, send_sem, recv_sem, to_g):
        return pltpu.make_async_remote_copy(
            src_ref=out.at[slot], dst_ref=out.at[slot], send_sem=send_sem,
            recv_sem=recv_sem, device_id=(to_g, d), device_id_type=MESH)

    def arrived(slot):
        pltpu.make_async_copy(out.at[slot], out.at[slot], slot_recv.at[slot]).wait()

    def to_core(slot):
        slot_copy(slot, core_send.at[0], core_recv.at[0], g_core).start()

    def source(j):
        i, k = lax.div(j, many), lax.rem(j, many)
        return (lax.rem(lax.div(d, many) + DIST // many - i, DIST // many) * many
                + lax.rem(lax.rem(d, many) + many - k, many))

    def from_dist(j):
        dd = source(j)
        slot = g * PER_GEO + dd

        @pl.when(dd < PER_GEO)
        def _():
            @pl.when(dd == d)
            def _():
                own_tile_copy().wait()

            @pl.when(dd != d)
            def _():
                arrived(slot)
            slot_copy(slot, right_send.at[0], slot_recv.at[slot], g_right).start()
            slot_copy(slot, left_send.at[0], slot_recv.at[slot], g_left).start()
            to_core(slot)

    def from_sides(j):
        dd = source(j)
        from_left, from_right = g_left * PER_GEO + dd, g_right * PER_GEO + dd

        @pl.when(dd < PER_GEO)
        def _():
            arrived(from_left)

            @pl.when(lax.rem(dd, 2) == 0)
            def _():
                slot_copy(from_left, right_send.at[1], slot_recv.at[from_left], g_right).start()
            to_core(from_left)
            arrived(from_right)

            @pl.when(lax.rem(dd, 2) == 1)
            def _():
                slot_copy(from_right, left_send.at[1], slot_recv.at[from_right], g_left).start()
            to_core(from_right)

    def from_far(j):
        dd = source(j)

        @pl.when(dd < PER_GEO)
        def _():
            arrived(g_far * PER_GEO + dd)
            to_core(g_far * PER_GEO + dd)

    def at_step(t, lag, body):
        j = t - lag

        @pl.when(jnp.logical_and(j >= 0, j < DIST))
        def _():
            body(j)

    def round_of(t, _):
        at_step(t, 0, from_dist)
        at_step(t, SIDE_LAG, from_sides)
        at_step(t, FAR_LAG, from_far)
        return 0
    lax.fori_loop(0, DIST + FAR_LAG, round_of, 0)

    def wait_slots(sem, n):
        ref = out.at[pl.ds(0, n)]
        pltpu.make_async_copy(ref, ref, sem).wait()
    wait_slots(core_recv.at[0], 4 * PER_GEO)
    wait_slots(core_send.at[0], 4 * PER_GEO)
    wait_slots(right_send.at[0], PER_GEO)
    wait_slots(left_send.at[0], PER_GEO)
    wait_slots(right_send.at[1], 8)
    wait_slots(left_send.at[1], 7)
    pltpu.make_async_copy(others, others, pk_send.at[0]).wait()

    @pl.when(mine)
    def _():
        wait_slots(tile_send.at[0], DIST - 1)
        ref = table.at[pl.ds(0, (SLOTS - 1) * ROWS), :]
        pltpu.make_async_copy(ref, ref, row_send.at[0]).wait()

    @pl.when(jnp.logical_not(mine))
    def _():
        ref = table.at[pl.ds(0, SLOTS * ROWS), :]
        pltpu.make_async_copy(ref, ref, row_send.at[0]).wait()


def tile_sums(idx, wgt, est, fac, var):
    vmem = pl.BlockSpec(memory_space=pltpu.VMEM)
    hbm = pl.BlockSpec(memory_space=pltpu.MemorySpace.HBM)
    dma = pltpu.SemaphoreType.DMA
    return pl.pallas_call(
        sums_kernel,
        out_shape=jax.ShapeDtypeStruct((SLOTS, CODE_ROWS, LANES), jnp.int16),
        in_specs=[vmem, vmem, hbm, hbm, vmem],
        out_specs=vmem,
        scratch_shapes=[
            pltpu.VMEM((DIST, INTER, DB), jnp.int32),
            pltpu.VMEM((ROWS, LANES), jnp.bfloat16),
            pltpu.VMEM((TRACTS, LANES), jnp.bfloat16),
            pltpu.VMEM((DIST, DB, LANES), jnp.bfloat16),
            pltpu.VMEM((DIST, DB, LANES), jnp.bfloat16),
            pltpu.VMEM((DIST, DB, LANES), jnp.float32),
            pltpu.VMEM((DIST, CODE_ROWS, LANES), jnp.int16),
            pltpu.SemaphoreType.REGULAR, dma(()), dma((1,)), dma((1,)), dma((1,)), dma((GEO,)),
            dma((1,)), dma((SLOTS,)), dma((2,)), dma((2,)), dma((1,)), dma((1,)),
        ],
        compiler_params=pltpu.CompilerParams(has_side_effects=True, collective_id=0, vmem_limit_bytes=40 * 2**20),
        name="tile_sums",
    )(idx, wgt, est, fac, var)


GROUP = 8
CROWS = 120
CHUNK = 4


def blocks_kernel(slots, marg_hbm, cov_hbm, loading, marg, noise, paired, outer, flat, marg_sem, cov_sem):
    def decode(slot):
        code = slots[slot, 0:DB, :].astype(jnp.int32).astype(jnp.float32)
        e = slots[slot, DB:CODE_ROWS, :].astype(jnp.int32).astype(jnp.float32)
        return code * (jnp.exp2(e[0:1, :]) * (1.0 / STEPS))

    for t in range(TABLE_TILES):
        marg[:, t * LANES:(t + 1) * LANES] = decode(t)
    out_marg = pltpu.make_async_copy(marg, marg_hbm, marg_sem)
    out_marg.start()

    noise[...] = jnp.transpose(decode(HI) + decode(LO) * (1.0 / 256.0))

    def load_tile(t, _):
        loading[pl.ds(pl.multiple_of(t * DB, DB), DB), :] = decode(TABLE_TILES + t)
        return 0
    lax.fori_loop(0, TABLE_TILES, load_tile, 0)

    paired[...] = jnp.zeros_like(paired)
    lane_row = lax.broadcasted_iota(jnp.int32, (TABLE_TILES, LANES), 1)
    lane_full = lax.broadcasted_iota(jnp.int32, (LANES, LANES), 1)
    sub = lax.broadcasted_iota(jnp.int32, (LANES, LANES), 0)

    def group(grp, _):
        for k in range(GROUP):
            rows = loading[pl.ds(grp * GROUP + k, TABLE_TILES, stride=DB), :]
            turned = pltpu.roll(rows, RANK, axis=1)
            low = lane_row < RANK
            paired[k, pl.ds(0, TABLE_TILES, stride=2), :] = jnp.where(low, rows, turned)
            paired[k, pl.ds(1, TABLE_TILES, stride=2), :] = jnp.where(low, turned, rows)
        for k in range(GROUP):
            full = paired[k]
            hi = full.astype(jnp.bfloat16)
            lo = (full - hi.astype(jnp.float32)).astype(jnp.bfloat16)
            mixed = jnp.where(lane_full < RANK, hi, lo)
            left = jnp.concatenate([mixed, mixed], axis=1)
            right = jnp.concatenate([hi, lo], axis=1)
            product = lax.dot_general(left, right, (((1,), (1,)), ((), ())), preferred_element_type=jnp.float32)
            outer[pl.ds(pl.multiple_of((grp * GROUP + k) * CROWS, 8), CROWS), :] = product[0:CROWS, :]
        return 0
    lax.fori_loop(0, DB // GROUP, group, 0)

    span = CHUNK * AGES

    def cov_copy(n):
        rows = pl.ds(pl.multiple_of(n * span, 8), span)
        return pltpu.make_async_copy(flat.at[rows, :], cov_hbm.at[rows, :], cov_sem)

    def ages(n, _):
        for pair in range(CHUNK // 2):
            halves = []
            for h in range(2):
                i = n * CHUNK + pair * 2 + h
                block = jnp.transpose(outer[pl.ds(i, DB, stride=CROWS), :])
                block = block + jnp.where(sub == i, noise[pl.ds(i, 1), :], 0.0)
                halves.append(block[0:AGES, :])
            flat[pl.ds(pl.multiple_of(n * span + pair * 2 * AGES, 8), 2 * AGES), :] = jnp.concatenate(halves, axis=0)
        cov_copy(n).start()
        return 0
    lax.fori_loop(0, AGES // CHUNK, ages, 0)
    pltpu.make_async_copy(flat, cov_hbm, cov_sem).wait()
    out_marg.wait()


def blocks(slots):
    vmem = pl.BlockSpec(memory_space=pltpu.VMEM)
    hbm = pl.BlockSpec(memory_space=pltpu.MemorySpace.HBM)
    dma = pltpu.SemaphoreType.DMA
    marg, cov = pl.pallas_call(
        blocks_kernel,
        out_shape=(jax.ShapeDtypeStruct((DB, TABLE_TILES * LANES), jnp.float32),
                   jax.ShapeDtypeStruct((AGES * AGES, DB), jnp.float32)),
        in_specs=[vmem],
        out_specs=(hbm, hbm),
        scratch_shapes=[
            pltpu.VMEM((TABLE_TILES * DB, LANES), jnp.float32),
            pltpu.VMEM((DB, TABLE_TILES * LANES), jnp.float32),
            pltpu.VMEM((DB, LANES), jnp.float32),
            pltpu.VMEM((GROUP, LANES, LANES), jnp.float32),
            pltpu.VMEM((DB * CROWS, LANES), jnp.float32),
            pltpu.VMEM((AGES * AGES, DB), jnp.float32),
            dma(()), dma(()),
        ],
        compiler_params=pltpu.CompilerParams(vmem_limit_bytes=48 * 2**20),
        name="district_blocks",
    )(slots)
    return marg, cov.T


def shards(estimates, factors, variances, intersection_tracts, intersection_weights):
    slots = tile_sums(intersection_tracts.T, intersection_weights.T, estimates, factors, variances)
    return blocks(slots)


def solution(mesh):
    return jax.shard_map(
        shards,
        mesh=mesh,
        in_specs=(
            P(("geo", "dist"), None),
            P(("geo", "dist"), None),
            P(("geo", "dist"), None),
            P("dist", None),
            P("dist", None),
        ),
        out_specs=(P("dist", None), P("dist", None)),
        check_vma=False,
    )
```

```python
import jax
import jax.numpy as jnp
from jax import lax
from jax.experimental import pallas as pl
from jax.experimental.pallas import tpu as pltpu
from jax.sharding import PartitionSpec as P

MESH = pl.DeviceIdType.MESH
GEO, DIST = 8, 16
DEVICES = GEO * DIST
LANES = 128
ROWS = 48
TRACTS = ROWS * DEVICES
BLOCK = ROWS * DIST
DB = 128
INTER = 32
WIDE = 2 * LANES
TABLE_TILES = 58
PAIRS = TABLE_TILES // 2
HI, LO = PAIRS, PAIRS + 1
PER_GEO = 15
HALF = DIST // 2
SLOTS = GEO * PER_GEO
CODE_ROWS = DB + 8
STEPS = 32000.0
AGES, RANK = 116, 64
SIDE_LAG, FAR_LAG = 8, 14
AHEAD = 4


def even_pair(x, d):
    return x * 8 + lax.div(d, 2)


def odd_pair(x, d):
    return x * 7 + lax.div(d, 2)


def factor_slot(t):
    f = t // 2
    return ((f // 8) * 2 + t % 2) * PER_GEO + 2 * (f % 8)


def estimate_slot(t):
    e = t // 2
    x, d = (3, 14) if e == PAIRS - 1 else (e // 7, 2 * (e % 7) + 1)
    return (x * 2 + t % 2) * PER_GEO + d


def sums_kernel(idx_hbm, wgt_hbm, est_hbm, fac_hbm, var_hbm, out,
                idx, wgt, est, fac, var, in_sem,
                pk, varp, table, weight, block, sums, coded,
                ready, own_sem, pk_send, pk_recv, row_send, row_recv, fwd_send, fwd_recv,
                tile_send, slot_recv, right_send, left_send, core_send, core_recv):
    g = lax.axis_index("geo")
    d = lax.axis_index("dist")
    me = g * DIST + d
    mine = d < PER_GEO
    x, c = lax.div(g, 2), lax.rem(g, 2)
    even = lax.rem(d, 2) == 0
    my_pair = even_pair(x, d)
    is_hi = jnp.logical_and(even, my_pair == HI)
    is_lo = jnp.logical_and(even, my_pair == LO)
    at_home = lax.div(d, HALF) == c
    g_right = lax.rem(x + 1, 4) * 2 + c
    g_left = lax.rem(x + 3, 4) * 2 + c
    g_far = lax.rem(x + 2, 4) * 2 + c
    g_core = x * 2 + (1 - c)

    barrier = pltpu.get_barrier_semaphore()
    for s in range(1, DIST):
        pl.semaphore_signal(barrier, inc=1, device_id=(g, lax.rem(d + s, DIST)), device_id_type=MESH)
    for s in range(1, GEO):
        pl.semaphore_signal(barrier, inc=1, device_id=(lax.rem(g + s, GEO), d), device_id_type=MESH)

    loads = [pltpu.make_async_copy(src, dst, in_sem.at[n]) for n, (src, dst) in enumerate(
        ((idx_hbm, idx), (wgt_hbm, wgt), (var_hbm, var), (est_hbm, est), (fac_hbm, fac)))]
    for load in loads:
        load.start()

    loads[0].wait()
    loads[1].wait()
    pk[d] = idx[...] * 512 + wgt[...]
    varp[...] = jnp.zeros_like(varp)
    loads[2].wait()
    varp[:, 0:AGES] = var[...]
    loads[3].wait()
    loads[4].wait()

    my_rows = table.at[pl.ds(pl.multiple_of(me * ROWS, 16), ROWS), :]

    def row_copy(xe, de, src, cols):
        return pltpu.make_async_remote_copy(
            src_ref=src.at[:, cols], dst_ref=my_rows, send_sem=row_send.at[0],
            recv_sem=row_recv.at[x], device_id=(xe * 2 + c, de), device_id_type=MESH)

    def of_pair(src, pair):
        return src, pl.ds(pl.multiple_of(pair * WIDE, WIDE), WIDE)

    def for_even(f, also, action):
        @pl.when(jnp.logical_and(also, f < PAIRS))
        def _():
            action(*of_pair(fac, f))

        @pl.when(jnp.logical_and(also, jnp.logical_and(f >= PAIRS, f <= LO)))
        def _():
            action(varp, pl.ds(0, WIDE))

        @pl.when(jnp.logical_and(also, f > LO))
        def _():
            action(*of_pair(est, PAIRS - 1))

    def own_rows(src, cols):
        pltpu.make_async_copy(src.at[:, cols], my_rows, row_recv.at[x]).start()
    for_even(my_pair, even, own_rows)

    @pl.when(jnp.logical_and(jnp.logical_not(even), mine))
    def _():
        own_rows(*of_pair(est, odd_pair(x, d)))

    pl.semaphore_wait(barrier, DIST - 1 + GEO - 1)
    for s in range(1, GEO):
        pl.semaphore_signal(ready, inc=1, device_id=(lax.rem(g + s, GEO), d), device_id_type=MESH)

    def pk_copy(slot, to):
        return pltpu.make_async_remote_copy(
            src_ref=pk.at[slot], dst_ref=pk.at[slot], send_sem=pk_send.at[0],
            recv_sem=pk_recv.at[0], device_id=(g, to), device_id_type=MESH)

    @pl.when(at_home)
    def _():
        def pk_start(s, _):
            pk_copy(d, lax.rem(d + s, DIST)).start()
            return 0
        lax.fori_loop(1, DIST, pk_start, 0)

    def rows_to(r):
        def one(k, _):
            spot = lax.rem(lax.div(d, 2) + k, HALF)
            de = 2 * spot
            xe = lax.rem(x + r + de, 4)
            other = jnp.logical_or(xe != x, de != d)
            for_even(even_pair(xe, de), other, lambda src, cols: row_copy(xe, de, src, cols).start())
            do = 2 * spot + 1
            xo = lax.rem(x + r + do, 4)

            @pl.when(jnp.logical_and(do < PER_GEO, jnp.logical_or(xo != x, do != d)))
            def _():
                row_copy(xo, do, *of_pair(est, odd_pair(xo, do))).start()
            return 0
        lax.fori_loop(0, HALF, one, 0)
    pl.semaphore_wait(ready, GEO - 1)
    for r in range(AHEAD):
        rows_to(r)

    def pk_wait(n, sem):
        ref = pk.at[pl.ds(0, n)]
        pltpu.make_async_copy(ref, ref, sem.at[0]).wait()

    @pl.when(at_home)
    def _():
        pk_wait(HALF - 1, pk_recv)

    @pl.when(jnp.logical_not(at_home))
    def _():
        pk_wait(HALF, pk_recv)
    lane = lax.broadcasted_iota(jnp.int32, (DB, LANES), 1)
    residue = lax.broadcasted_iota(jnp.int32, (64, DB), 0)

    def weights_of(n, _):
        entries = pk[c * HALF + n]
        res = lax.shift_right_logical(entries, 9) & 63
        val = (lax.shift_right_logical(entries, 15) * 512) + (entries & 511)
        acc = jnp.zeros((64, DB), jnp.int32)
        for k in range(INTER):
            acc = jnp.where(residue == res[k:k + 1, :], val[k:k + 1, :], acc)
        both = jnp.transpose(jnp.concatenate([acc, acc], axis=0))
        w = both & 511
        square = w * w
        w = jnp.where(is_hi, lax.shift_right_logical(square, 8), jnp.where(is_lo, square & 255, w))
        b = lax.shift_right_logical(both, 9) - jnp.where(lane >= 64, 1, 0)
        weight[n] = (w.astype(jnp.float32) * (1.0 / 256.0)).astype(jnp.bfloat16)
        block[n] = b.astype(jnp.float32).astype(jnp.bfloat16)
        return 0
    lax.fori_loop(0, HALF, weights_of, 0)

    many = 4

    def product(q, gb):
        w = weight[pl.ds(q * many, many)].reshape(many * DB, LANES)
        b = block[pl.ds(q * many, many)].reshape(many * DB, LANES)
        zero = jnp.zeros_like(w)
        total = None
        for step in range(BLOCK // 256):
            parts = []
            for h in range(2):
                at = (2 * (gb * (BLOCK // LANES) + 2 * step + h)).astype(jnp.float32).astype(jnp.bfloat16)
                parts.append(jnp.where(b == at, w, zero))
            rows = table[pl.ds(pl.multiple_of(gb * BLOCK + step * 256, 256), 256), :]
            part = jnp.dot(jnp.concatenate(parts, axis=1), rows, preferred_element_type=jnp.float32)
            total = part if total is None else total + part
        return total.reshape(many, DB, WIDE)

    def tile_copy(n, h):
        slot = (x * 2 + h) * PER_GEO + d
        return pltpu.make_async_remote_copy(
            src_ref=coded.at[n, h], dst_ref=out.at[slot], send_sem=tile_send.at[0],
            recv_sem=slot_recv.at[slot], device_id=(x * 2 + h, c * HALF + n), device_id_type=MESH)

    def own_tile_copy():
        return pltpu.make_async_copy(coded.at[d - c * HALF, c], out.at[g * PER_GEO + d], own_sem)

    def encode(n):
        for h in range(2):
            total = sums[n, :, h * LANES:(h + 1) * LANES]
            top = jnp.maximum(jnp.max(jnp.abs(total), axis=0, keepdims=True), 1e-30)
            e = jnp.ceil(jnp.log2(top))
            code = jnp.round(total * (STEPS / jnp.exp2(e)))
            coded[n, h, 0:DB, :] = code.astype(jnp.int32).astype(jnp.int16)
            coded[n, h, DB:CODE_ROWS, :] = jnp.broadcast_to(e, (8, LANES)).astype(jnp.int32).astype(jnp.int16)

    first = lax.rem(lax.div(d, many), 2)

    def add_block(gb, start, finish):
        def part(i, _):
            q = lax.rem(first + i, 2)

            @pl.when(start)
            def _():
                sums[pl.ds(q * many, many)] = product(q, gb)

            @pl.when(jnp.logical_not(start))
            def _():
                sums[pl.ds(q * many, many)] += product(q, gb)

            @pl.when(finish)
            def _():
                for k in range(many):
                    n = q * many + lax.rem(lax.rem(d, many) + k, many)
                    encode(n)
                    for h in range(2):
                        own = jnp.logical_and(c * HALF + n == d, c == h)

                        @pl.when(jnp.logical_not(own))
                        def _():
                            tile_copy(n, h).start()

                        @pl.when(own)
                        def _():
                            own_tile_copy().start()
            return 0
        lax.fori_loop(0, 2, part, 0)

    def block_at(gb):
        return table.at[pl.ds(pl.multiple_of(gb * BLOCK, 256), BLOCK), :]

    def pass_on(xs):
        rows = block_at(xs * 2 + c)
        return pltpu.make_async_remote_copy(
            src_ref=rows, dst_ref=rows, send_sem=fwd_send.at[0], recv_sem=fwd_recv.at[xs],
            device_id=(g_core, d), device_id_type=MESH)

    def block_of(r, _):
        xs = lax.rem(x + 8 - lax.rem(d, 4) - r, 4)

        @pl.when(mine)
        def _():
            rows = block_at(xs * 2 + c)
            pltpu.make_async_copy(rows, rows, row_recv.at[xs]).wait()
            pass_on(xs).start()

        @pl.when(r < 4 - AHEAD)
        def _():
            rows_to(r + AHEAD)

        @pl.when(mine)
        def _():
            add_block(xs * 2 + c, r == 0, r < 0)
            rows = block_at(xs * 2 + 1 - c)
            pltpu.make_async_copy(rows, rows, fwd_recv.at[xs]).wait()
            add_block(xs * 2 + 1 - c, r < 0, r == 3)
        return 0
    lax.fori_loop(0, 4, block_of, 0)

    def slot_copy(slot, send_sem, recv_sem, to_g):
        return pltpu.make_async_remote_copy(
            src_ref=out.at[slot], dst_ref=out.at[slot], send_sem=send_sem,
            recv_sem=recv_sem, device_id=(to_g, d), device_id_type=MESH)

    def arrived(slot):
        pltpu.make_async_copy(out.at[slot], out.at[slot], slot_recv.at[slot]).wait()

    def to_core(slot):
        slot_copy(slot, core_send.at[0], core_recv.at[0], g_core).start()

    def source(j):
        odd = lax.div(j, 8)
        i, m, b = lax.rem(lax.div(j, 4), 2), lax.rem(lax.div(j, 2), 2), lax.rem(j, 2)
        k = 2 * m + lax.rem(d + odd, 2)
        return b * HALF + lax.rem(first + i, 2) * many + lax.rem(lax.rem(d, many) + many - k, many)

    def from_dist(j):
        dd = source(j)
        slot = g * PER_GEO + dd

        @pl.when(dd < PER_GEO)
        def _():
            own = jnp.logical_and(dd == d, at_home)

            @pl.when(own)
            def _():
                own_tile_copy().wait()

            @pl.when(jnp.logical_not(own))
            def _():
                arrived(slot)
            slot_copy(slot, right_send.at[0], slot_recv.at[slot], g_right).start()
            slot_copy(slot, left_send.at[0], slot_recv.at[slot], g_left).start()
            to_core(slot)

    def from_sides(j):
        dd = source(j)
        from_left, from_right = g_left * PER_GEO + dd, g_right * PER_GEO + dd

        @pl.when(dd < PER_GEO)
        def _():
            arrived(from_left)

            @pl.when(lax.rem(lax.div(dd, 2), 2) == 0)
            def _():
                slot_copy(from_left, right_send.at[1], slot_recv.at[from_left], g_right).start()
            to_core(from_left)
            arrived(from_right)

            @pl.when(lax.rem(lax.div(dd, 2), 2) == 1)
            def _():
                slot_copy(from_right, left_send.at[1], slot_recv.at[from_right], g_left).start()
            to_core(from_right)

    def from_far(j):
        dd = source(j)

        @pl.when(dd < PER_GEO)
        def _():
            arrived(g_far * PER_GEO + dd)
            to_core(g_far * PER_GEO + dd)

    def at_step(t, lag, body):
        j = t - lag

        @pl.when(jnp.logical_and(j >= 0, j < DIST))
        def _():
            body(j)

    def round_of(t, _):
        at_step(t, 0, from_dist)
        at_step(t, SIDE_LAG, from_sides)
        at_step(t, FAR_LAG, from_far)
        return 0
    lax.fori_loop(0, DIST + FAR_LAG, round_of, 0)

    def wait_slots(sem, n):
        ref = out.at[pl.ds(0, n)]
        pltpu.make_async_copy(ref, ref, sem).wait()
    wait_slots(core_recv.at[0], 4 * PER_GEO)
    wait_slots(core_send.at[0], 4 * PER_GEO)
    wait_slots(right_send.at[0], PER_GEO)
    wait_slots(left_send.at[0], PER_GEO)
    wait_slots(right_send.at[1], 8)
    wait_slots(left_send.at[1], 7)

    @pl.when(at_home)
    def _():
        pk_wait(DIST - 1, pk_send)

    def wait_rows(sem, n):
        ref = table.at[pl.ds(0, n), :]
        pltpu.make_async_copy(ref, ref, sem.at[0]).wait()

    @pl.when(mine)
    def _():
        wait_rows(row_send, (4 * PER_GEO - 1) * ROWS)
        wait_rows(fwd_send, 4 * BLOCK)

        @pl.when(at_home)
        def _():
            wait_slots(tile_send.at[0], DIST - 1)

        @pl.when(jnp.logical_not(at_home))
        def _():
            wait_slots(tile_send.at[0], DIST)

    @pl.when(jnp.logical_not(mine))
    def _():
        wait_rows(row_send, 4 * PER_GEO * ROWS)


def tile_sums(idx, wgt, est, fac, var):
    vmem = pl.BlockSpec(memory_space=pltpu.VMEM)
    hbm = pl.BlockSpec(memory_space=pltpu.MemorySpace.HBM)
    dma = pltpu.SemaphoreType.DMA
    return pl.pallas_call(
        sums_kernel,
        out_shape=jax.ShapeDtypeStruct((SLOTS, CODE_ROWS, LANES), jnp.int16),
        in_specs=[hbm] * 5,
        out_specs=vmem,
        scratch_shapes=[
            pltpu.VMEM((INTER, DB), jnp.int32),
            pltpu.VMEM((INTER, DB), jnp.int32),
            pltpu.VMEM(est.shape, jnp.bfloat16),
            pltpu.VMEM(fac.shape, jnp.bfloat16),
            pltpu.VMEM(var.shape, jnp.bfloat16),
            dma((5,)),
            pltpu.VMEM((DIST, INTER, DB), jnp.int32),
            pltpu.VMEM((ROWS, WIDE), jnp.bfloat16),
            pltpu.VMEM((TRACTS, WIDE), jnp.bfloat16),
            pltpu.VMEM((HALF, DB, LANES), jnp.bfloat16),
            pltpu.VMEM((HALF, DB, LANES), jnp.bfloat16),
            pltpu.VMEM((HALF, DB, WIDE), jnp.float32),
            pltpu.VMEM((HALF, 2, CODE_ROWS, LANES), jnp.int16),
            pltpu.SemaphoreType.REGULAR, dma(()), dma((1,)), dma((1,)), dma((1,)), dma((4,)), dma((1,)), dma((4,)),
            dma((1,)), dma((SLOTS,)), dma((2,)), dma((2,)), dma((1,)), dma((1,)),
        ],
        compiler_params=pltpu.CompilerParams(has_side_effects=True, collective_id=0, vmem_limit_bytes=40 * 2**20),
        name="tile_sums",
    )(idx, wgt, est, fac, var)


GROUP = 8
CROWS = 120
CHUNK = 4


def blocks_kernel(slots, marg_hbm, cov_hbm, loading, marg, noise, paired, outer, flat, marg_sem, cov_sem):
    def decode(slot):
        code = slots[slot, 0:DB, :].astype(jnp.int32).astype(jnp.float32)
        e = slots[slot, DB:CODE_ROWS, :].astype(jnp.int32).astype(jnp.float32)
        return code * (jnp.exp2(e[0:1, :]) * (1.0 / STEPS))

    for t in range(TABLE_TILES):
        marg[:, t * LANES:(t + 1) * LANES] = decode(estimate_slot(t))
    out_marg = pltpu.make_async_copy(marg, marg_hbm, marg_sem)
    out_marg.start()

    noise[...] = jnp.transpose(decode(factor_slot(2 * HI)) + decode(factor_slot(2 * LO)) * (1.0 / 256.0))

    for t in range(TABLE_TILES):
        loading[t * DB:(t + 1) * DB, :] = decode(factor_slot(t))

    paired[...] = jnp.zeros_like(paired)
    lane_row = lax.broadcasted_iota(jnp.int32, (TABLE_TILES, LANES), 1)
    lane_full = lax.broadcasted_iota(jnp.int32, (LANES, LANES), 1)
    sub = lax.broadcasted_iota(jnp.int32, (LANES, LANES), 0)

    def group(grp, _):
        for k in range(GROUP):
            rows = loading[pl.ds(grp * GROUP + k, TABLE_TILES, stride=DB), :]
            turned = pltpu.roll(rows, RANK, axis=1)
            low = lane_row < RANK
            paired[k, pl.ds(0, TABLE_TILES, stride=2), :] = jnp.where(low, rows, turned)
            paired[k, pl.ds(1, TABLE_TILES, stride=2), :] = jnp.where(low, turned, rows)
        for k in range(GROUP):
            full = paired[k]
            hi = full.astype(jnp.bfloat16)
            lo = (full - hi.astype(jnp.float32)).astype(jnp.bfloat16)
            mixed = jnp.where(lane_full < RANK, hi, lo)
            left = jnp.concatenate([mixed, mixed], axis=1)
            right = jnp.concatenate([hi, lo], axis=1)
            product = lax.dot_general(left, right, (((1,), (1,)), ((), ())), preferred_element_type=jnp.float32)
            outer[pl.ds(pl.multiple_of((grp * GROUP + k) * CROWS, 8), CROWS), :] = product[0:CROWS, :]
        return 0
    lax.fori_loop(0, DB // GROUP, group, 0)

    span = CHUNK * AGES

    def cov_copy(n):
        rows = pl.ds(pl.multiple_of(n * span, 8), span)
        return pltpu.make_async_copy(flat.at[rows, :], cov_hbm.at[rows, :], cov_sem)

    def ages(n, _):
        for pair in range(CHUNK // 2):
            halves = []
            for h in range(2):
                i = n * CHUNK + pair * 2 + h
                block = jnp.transpose(outer[pl.ds(i, DB, stride=CROWS), :])
                block = block + jnp.where(sub == i, noise[pl.ds(i, 1), :], 0.0)
                halves.append(block[0:AGES, :])
            flat[pl.ds(pl.multiple_of(n * span + pair * 2 * AGES, 8), 2 * AGES), :] = jnp.concatenate(halves, axis=0)
        cov_copy(n).start()
        return 0
    lax.fori_loop(0, AGES // CHUNK, ages, 0)
    pltpu.make_async_copy(flat, cov_hbm, cov_sem).wait()
    out_marg.wait()


def blocks(slots):
    vmem = pl.BlockSpec(memory_space=pltpu.VMEM)
    hbm = pl.BlockSpec(memory_space=pltpu.MemorySpace.HBM)
    dma = pltpu.SemaphoreType.DMA
    marg, cov = pl.pallas_call(
        blocks_kernel,
        out_shape=(jax.ShapeDtypeStruct((DB, TABLE_TILES * LANES), jnp.float32),
                   jax.ShapeDtypeStruct((AGES * AGES, DB), jnp.float32)),
        in_specs=[vmem],
        out_specs=(hbm, hbm),
        scratch_shapes=[
            pltpu.VMEM((TABLE_TILES * DB, LANES), jnp.float32),
            pltpu.VMEM((DB, TABLE_TILES * LANES), jnp.float32),
            pltpu.VMEM((DB, LANES), jnp.float32),
            pltpu.VMEM((GROUP, LANES, LANES), jnp.float32),
            pltpu.VMEM((DB * CROWS, LANES), jnp.float32),
            pltpu.VMEM((AGES * AGES, DB), jnp.float32),
            dma(()), dma(()),
        ],
        compiler_params=pltpu.CompilerParams(vmem_limit_bytes=48 * 2**20),
        name="district_blocks",
    )(slots)
    return marg, cov.T


def shards(estimates, factors, variances, intersection_tracts, intersection_weights):
    keep = lambda a: pltpu.with_memory_space_constraint(a, pltpu.MemorySpace.HBM)
    slots = tile_sums(keep(intersection_tracts.T), keep(intersection_weights.T), keep(estimates), keep(factors), keep(variances))
    return blocks(slots)


def solution(mesh):
    return jax.shard_map(
        shards,
        mesh=mesh,
        in_specs=(
            P(("geo", "dist"), None),
            P(("geo", "dist"), None),
            P(("geo", "dist"), None),
            P("dist", None),
            P("dist", None),
        ),
        out_specs=(P("dist", None), P("dist", None)),
        check_vma=False,
    )
```

```python
import jax
import jax.numpy as jnp
from jax import lax
from jax.experimental import pallas as pl
from jax.experimental.pallas import tpu as pltpu
from jax.sharding import PartitionSpec as P

MESH = pl.DeviceIdType.MESH
GEO, DIST = 8, 16
DEVICES = GEO * DIST
LANES = 128
ROWS = 48
TRACTS = ROWS * DEVICES
BLOCK = ROWS * DIST
DB = 128
INTER = 32
TABLE_TILES = 58
HI, LO = TABLE_TILES, TABLE_TILES + 1
PER_X = 15
CHIPS = 4 * PER_X
HALF = DIST // 2
SLOTS = 2 * CHIPS
CODE_ROWS = DB + 8
STEPS = 32000.0
AGES, RANK = 116, 64
AHEAD = 3


def sums_kernel(idx_hbm, wgt_hbm, est_hbm, fac_hbm, var_hbm, out,
                idx, wgt, est, fac, var, in_sem,
                pk, varp, table, weight, block, sums, coded,
                ready, own_sem, pk_send, pk_recv, row_send, row_recv, fwd_send, fwd_recv,
                tile_send, slot_recv, right_send, left_send, core_send, core_recv):
    g = lax.axis_index("geo")
    d = lax.axis_index("dist")
    me = g * DIST + d
    mine = d < PER_X
    x, c = lax.div(g, 2), lax.rem(g, 2)
    my_tile = x * PER_X + d
    at_home = lax.div(d, HALF) == c
    g_right = lax.rem(x + 1, 4) * 2 + c
    g_left = lax.rem(x + 3, 4) * 2 + c
    g_far = lax.rem(x + 2, 4) * 2 + c
    g_core = x * 2 + (1 - c)

    barrier = pltpu.get_barrier_semaphore()
    for s in range(1, DIST):
        pl.semaphore_signal(barrier, inc=1, device_id=(g, lax.rem(d + s, DIST)), device_id_type=MESH)
    for s in range(1, GEO):
        pl.semaphore_signal(barrier, inc=1, device_id=(lax.rem(g + s, GEO), d), device_id_type=MESH)

    loads = [pltpu.make_async_copy(src, dst, in_sem.at[n]) for n, (src, dst) in enumerate(
        ((idx_hbm, idx), (wgt_hbm, wgt), (var_hbm, var), (est_hbm, est), (fac_hbm, fac)))]
    for load in loads:
        load.start()

    loads[0].wait()
    loads[1].wait()
    pk[d] = idx[...] * 512 + wgt[...]
    varp[...] = jnp.zeros_like(varp)
    loads[2].wait()
    varp[:, 0:AGES] = var[...]
    loads[3].wait()
    loads[4].wait()

    my_range = pl.ds(pl.multiple_of(me * ROWS, 16), ROWS)
    sources = (fac, est)

    def for_tile(kind, t, also, action):
        @pl.when(jnp.logical_and(also, t < TABLE_TILES))
        def _():
            action(sources[kind].at[:, pl.ds(pl.multiple_of(t * LANES, LANES), LANES)])

        @pl.when(jnp.logical_and(also, t >= TABLE_TILES))
        def _():
            action(varp)

    for kind in range(2):
        for_tile(kind, my_tile, mine, lambda src: pltpu.make_async_copy(
            src, table.at[kind, my_range, :], row_recv.at[kind * 4 + x]).start())

    pl.semaphore_wait(barrier, DIST - 1 + GEO - 1)
    for s in range(1, GEO):
        pl.semaphore_signal(ready, inc=1, device_id=(lax.rem(g + s, GEO), d), device_id_type=MESH)

    def pk_copy(slot, to):
        return pltpu.make_async_remote_copy(
            src_ref=pk.at[slot], dst_ref=pk.at[slot], send_sem=pk_send.at[0],
            recv_sem=pk_recv.at[0], device_id=(g, to), device_id_type=MESH)

    @pl.when(at_home)
    def _():
        def pk_start(s, _):
            pk_copy(d, lax.rem(d + s, DIST)).start()
            return 0
        lax.fori_loop(1, DIST, pk_start, 0)

    def rows_to(kind, r):
        def one(k, _):
            de = lax.rem(d + k, DIST)
            xe = lax.rem(x + r + de, 4)
            other = jnp.logical_and(de < PER_X, jnp.logical_or(xe != x, de != d))
            for_tile(kind, xe * PER_X + de, other, lambda src: pltpu.make_async_remote_copy(
                src_ref=src, dst_ref=table.at[kind, my_range, :], send_sem=row_send.at[kind],
                recv_sem=row_recv.at[kind * 4 + x], device_id=(xe * 2 + c, de), device_id_type=MESH).start())
            return 0
        lax.fori_loop(0, DIST, one, 0)
    pl.semaphore_wait(ready, GEO - 1)
    for r in range(AHEAD):
        rows_to(0, r)

    def pk_wait(n, sem):
        ref = pk.at[pl.ds(0, n)]
        pltpu.make_async_copy(ref, ref, sem.at[0]).wait()

    @pl.when(at_home)
    def _():
        pk_wait(HALF - 1, pk_recv)

    @pl.when(jnp.logical_not(at_home))
    def _():
        pk_wait(HALF, pk_recv)
    lane = lax.broadcasted_iota(jnp.int32, (DB, LANES), 1)
    residue = lax.broadcasted_iota(jnp.int32, (64, DB), 0)

    def weights_of(n, _):
        entries = pk[c * HALF + n]
        res = lax.shift_right_logical(entries, 9) & 63
        val = (lax.shift_right_logical(entries, 15) * 512) + (entries & 511)
        acc = jnp.zeros((64, DB), jnp.int32)
        for k in range(INTER):
            acc = jnp.where(residue == res[k:k + 1, :], val[k:k + 1, :], acc)
        both = jnp.transpose(jnp.concatenate([acc, acc], axis=0))
        w = both & 511
        square = w * w
        w = jnp.where(my_tile == HI, lax.shift_right_logical(square, 8), jnp.where(my_tile == LO, square & 255, w))
        b = lax.shift_right_logical(both, 9) - jnp.where(lane >= 64, 1, 0)
        weight[n] = (w.astype(jnp.float32) * (1.0 / 256.0)).astype(jnp.bfloat16)
        block[n] = b.astype(jnp.float32).astype(jnp.bfloat16)
        return 0
    lax.fori_loop(0, HALF, weights_of, 0)

    many = 4

    def add_block(kind, gb):
        def part(q, _):
            w = weight[pl.ds(q * many, many)].reshape(many * DB, LANES)
            b = block[pl.ds(q * many, many)].reshape(many * DB, LANES)
            zero = jnp.zeros_like(w)
            total = None
            for step in range(BLOCK // 256):
                parts = []
                for h in range(2):
                    at = (2 * (gb * (BLOCK // LANES) + 2 * step + h)).astype(jnp.float32).astype(jnp.bfloat16)
                    parts.append(jnp.where(b == at, w, zero))
                rows = table[kind, pl.ds(pl.multiple_of(gb * BLOCK + step * 256, 256), 256), :]
                product = jnp.dot(jnp.concatenate(parts, axis=1), rows, preferred_element_type=jnp.float32)
                total = product if total is None else total + product
            sums[pl.ds(q * many, many)] += total.reshape(many, DB, LANES)
            return 0
        lax.fori_loop(0, HALF // many, part, 0)

    def block_rows(kind, gb):
        return table.at[kind, pl.ds(pl.multiple_of(gb * BLOCK, 256), BLOCK), :]

    def phase(kind, r, then):
        xs = lax.rem(x + 8 - lax.rem(d, 4) - r, 4)
        n = kind * 4 + xs
        own, other = xs * 2 + c, xs * 2 + 1 - c

        @pl.when(mine)
        def _():
            rows = block_rows(kind, own)
            pltpu.make_async_copy(rows, rows, row_recv.at[n]).wait()
            pltpu.make_async_remote_copy(
                src_ref=rows, dst_ref=rows, send_sem=fwd_send.at[kind], recv_sem=fwd_recv.at[n],
                device_id=(g_core, d), device_id_type=MESH).start()
        then()

        @pl.when(mine)
        def _():
            add_block(kind, own)
            rows = block_rows(kind, other)
            pltpu.make_async_copy(rows, rows, fwd_recv.at[n]).wait()
            add_block(kind, other)

    def side_of(kind, dd):
        return lax.rem(dd + kind, 2)

    def tile_copy(kind, n):
        slot = kind * CHIPS + my_tile
        return pltpu.make_async_remote_copy(
            src_ref=coded.at[kind, n], dst_ref=out.at[slot], send_sem=tile_send.at[kind], recv_sem=slot_recv.at[slot],
            device_id=(x * 2 + side_of(kind, d), c * HALF + n), device_id_type=MESH)

    def own_tile_copy(kind):
        return pltpu.make_async_copy(coded.at[kind, d - c * HALF], out.at[kind * CHIPS + my_tile], own_sem.at[kind])

    def stays(kind, dd):
        return jnp.logical_and(jnp.logical_and(dd == d, at_home), side_of(kind, d) == c)

    first = lax.rem(lax.div(d, many), 2)

    def encode(kind):
        def one(i, _):
            n = lax.rem(first + lax.div(i, many), 2) * many + lax.rem(d + i, many)
            total = sums[n]
            top = jnp.maximum(jnp.max(jnp.abs(total), axis=0, keepdims=True), 1e-30)
            e = jnp.ceil(jnp.log2(top))
            code = jnp.round(total * (STEPS / jnp.exp2(e)))
            coded[kind, n, 0:DB, :] = code.astype(jnp.int32).astype(jnp.int16)
            coded[kind, n, DB:CODE_ROWS, :] = jnp.broadcast_to(e, (8, LANES)).astype(jnp.int32).astype(jnp.int16)
            own = stays(kind, c * HALF + n)

            @pl.when(jnp.logical_not(own))
            def _():
                tile_copy(kind, n).start()

            @pl.when(own)
            def _():
                own_tile_copy(kind).start()
            return 0
        lax.fori_loop(0, HALF, one, 0)
        sums[...] = jnp.zeros_like(sums)

    def slot_copy(slot, send_sem, recv_sem, to_g):
        return pltpu.make_async_remote_copy(
            src_ref=out.at[slot], dst_ref=out.at[slot], send_sem=send_sem,
            recv_sem=recv_sem, device_id=(to_g, d), device_id_type=MESH)

    def arrived(slot):
        pltpu.make_async_copy(out.at[slot], out.at[slot], slot_recv.at[slot]).wait()

    def to_core(kind, slot):
        slot_copy(slot, core_send.at[0], core_recv.at[kind], g_core).start()

    def source(kind, j):
        i, m, b = lax.div(j, 4), lax.rem(lax.div(j, 2), 2), lax.rem(j, 2)
        k = 2 * m + lax.rem(d + c + kind, 2)
        return b * HALF + lax.rem(first + i, 2) * many + lax.rem(lax.rem(d, many) + many - k, many)

    def slot_at(kind, xx, dd):
        return kind * CHIPS + xx * PER_X + dd

    def from_dist(kind, j):
        dd = source(kind, j)
        slot = slot_at(kind, x, dd)

        @pl.when(dd < PER_X)
        def _():
            own = stays(kind, dd)

            @pl.when(own)
            def _():
                own_tile_copy(kind).wait()

            @pl.when(jnp.logical_not(own))
            def _():
                arrived(slot)
            slot_copy(slot, right_send.at[0], slot_recv.at[slot], g_right).start()
            slot_copy(slot, left_send.at[0], slot_recv.at[slot], g_left).start()
            to_core(kind, slot)

    def from_sides(kind, j):
        dd = source(kind, j)
        from_left = slot_at(kind, lax.rem(x + 3, 4), dd)
        from_right = slot_at(kind, lax.rem(x + 1, 4), dd)

        @pl.when(dd < PER_X)
        def _():
            arrived(from_left)

            @pl.when(lax.rem(lax.div(dd, 2), 2) == 0)
            def _():
                slot_copy(from_left, right_send.at[1], slot_recv.at[from_left], g_right).start()
            to_core(kind, from_left)
            arrived(from_right)

            @pl.when(lax.rem(lax.div(dd, 2), 2) == 1)
            def _():
                slot_copy(from_right, left_send.at[1], slot_recv.at[from_right], g_left).start()
            to_core(kind, from_right)

    def from_far(kind, j):
        dd = source(kind, j)

        @pl.when(dd < PER_X)
        def _():
            slot = slot_at(kind, lax.rem(x + 2, 4), dd)
            arrived(slot)
            to_core(kind, slot)

    def many_of(body, kind, start, stop):
        def one(j, _):
            body(kind, j)
            return 0
        lax.fori_loop(start, stop, one, 0)

    sums[...] = jnp.zeros_like(sums)
    for n in range(8):
        kind, r = n // 4, n % 4

        def then():
            if n + AHEAD < 8:
                rows_to((n + AHEAD) // 4, (n + AHEAD) % 4)
        phase(kind, r, then)
        if r == 3:
            @pl.when(mine)
            def _():
                encode(kind)
        if n == 5:
            many_of(from_dist, 0, 0, 4)
        if n == 6:
            many_of(from_dist, 0, 4, 8)
    many_of(from_sides, 0, 0, 8)
    many_of(from_dist, 1, 0, 8)
    many_of(from_far, 0, 0, 8)
    many_of(from_sides, 1, 0, 8)
    many_of(from_far, 1, 0, 8)

    def wait_slots(sem, n):
        ref = out.at[pl.ds(0, n)]
        pltpu.make_async_copy(ref, ref, sem).wait()
    odd_side = jnp.where(c == 1, 1, 0)
    for kind in range(2):
        @pl.when(odd_side == 1 - kind)
        def _():
            wait_slots(core_recv.at[kind], 4 * 8)

        @pl.when(odd_side == kind)
        def _():
            wait_slots(core_recv.at[kind], 4 * 7)
    wait_slots(core_send.at[0], 4 * PER_X)
    wait_slots(right_send.at[0], PER_X)
    wait_slots(left_send.at[0], PER_X)
    wait_slots(right_send.at[1], 8)
    wait_slots(left_send.at[1], 7)

    @pl.when(at_home)
    def _():
        pk_wait(DIST - 1, pk_send)

    for kind in range(2):
        def wait_rows(sem, n):
            ref = table.at[kind, pl.ds(0, n), :]
            pltpu.make_async_copy(ref, ref, sem.at[kind]).wait()

        @pl.when(mine)
        def _():
            wait_rows(row_send, (CHIPS - 1) * ROWS)
            wait_rows(fwd_send, 4 * BLOCK)
            own = stays(kind, d)

            @pl.when(own)
            def _():
                wait_slots(tile_send.at[kind], HALF - 1)

            @pl.when(jnp.logical_not(own))
            def _():
                wait_slots(tile_send.at[kind], HALF)

        @pl.when(jnp.logical_not(mine))
        def _():
            wait_rows(row_send, CHIPS * ROWS)


def tile_sums(idx, wgt, est, fac, var):
    vmem = pl.BlockSpec(memory_space=pltpu.VMEM)
    hbm = pl.BlockSpec(memory_space=pltpu.MemorySpace.HBM)
    dma = pltpu.SemaphoreType.DMA
    return pl.pallas_call(
        sums_kernel,
        out_shape=jax.ShapeDtypeStruct((SLOTS, CODE_ROWS, LANES), jnp.int16),
        in_specs=[hbm] * 5,
        out_specs=vmem,
        scratch_shapes=[
            pltpu.VMEM((INTER, DB), jnp.int32),
            pltpu.VMEM((INTER, DB), jnp.int32),
            pltpu.VMEM(est.shape, jnp.bfloat16),
            pltpu.VMEM(fac.shape, jnp.bfloat16),
            pltpu.VMEM(var.shape, jnp.bfloat16),
            dma((5,)),
            pltpu.VMEM((DIST, INTER, DB), jnp.int32),
            pltpu.VMEM((ROWS, LANES), jnp.bfloat16),
            pltpu.VMEM((2, TRACTS, LANES), jnp.bfloat16),
            pltpu.VMEM((HALF, DB, LANES), jnp.bfloat16),
            pltpu.VMEM((HALF, DB, LANES), jnp.bfloat16),
            pltpu.VMEM((HALF, DB, LANES), jnp.float32),
            pltpu.VMEM((2, HALF, CODE_ROWS, LANES), jnp.int16),
            pltpu.SemaphoreType.REGULAR, dma((2,)), dma((1,)), dma((1,)), dma((2,)), dma((8,)), dma((2,)), dma((8,)),
            dma((2,)), dma((SLOTS,)), dma((2,)), dma((2,)), dma((1,)), dma((2,)),
        ],
        compiler_params=pltpu.CompilerParams(has_side_effects=True, collective_id=0, vmem_limit_bytes=40 * 2**20),
        name="tile_sums",
    )(idx, wgt, est, fac, var)


GROUP = 8
CROWS = 120
CHUNK = 4


def blocks_kernel(slots, marg_hbm, cov_hbm, loading, marg, noise, paired, outer, flat, marg_sem, cov_sem):
    def decode(slot):
        code = slots[slot, 0:DB, :].astype(jnp.int32).astype(jnp.float32)
        e = slots[slot, DB:CODE_ROWS, :].astype(jnp.int32).astype(jnp.float32)
        return code * (jnp.exp2(e[0:1, :]) * (1.0 / STEPS))

    for t in range(TABLE_TILES):
        marg[:, t * LANES:(t + 1) * LANES] = decode(CHIPS + t)
    out_marg = pltpu.make_async_copy(marg, marg_hbm, marg_sem)
    out_marg.start()

    noise[...] = jnp.transpose(decode(HI) + decode(LO) * (1.0 / 256.0))

    for t in range(TABLE_TILES):
        loading[t * DB:(t + 1) * DB, :] = decode(t)

    paired[...] = jnp.zeros_like(paired)
    lane_row = lax.broadcasted_iota(jnp.int32, (TABLE_TILES, LANES), 1)
    lane_full = lax.broadcasted_iota(jnp.int32, (LANES, LANES), 1)
    sub = lax.broadcasted_iota(jnp.int32, (LANES, LANES), 0)

    def group(grp, _):
        for k in range(GROUP):
            rows = loading[pl.ds(grp * GROUP + k, TABLE_TILES, stride=DB), :]
            turned = pltpu.roll(rows, RANK, axis=1)
            low = lane_row < RANK
            paired[k, pl.ds(0, TABLE_TILES, stride=2), :] = jnp.where(low, rows, turned)
            paired[k, pl.ds(1, TABLE_TILES, stride=2), :] = jnp.where(low, turned, rows)
        for k in range(GROUP):
            full = paired[k]
            hi = full.astype(jnp.bfloat16)
            lo = (full - hi.astype(jnp.float32)).astype(jnp.bfloat16)
            mixed = jnp.where(lane_full < RANK, hi, lo)
            left = jnp.concatenate([mixed, mixed], axis=1)
            right = jnp.concatenate([hi, lo], axis=1)
            product = lax.dot_general(left, right, (((1,), (1,)), ((), ())), preferred_element_type=jnp.float32)
            outer[pl.ds(pl.multiple_of((grp * GROUP + k) * CROWS, 8), CROWS), :] = product[0:CROWS, :]
        return 0
    lax.fori_loop(0, DB // GROUP, group, 0)

    span = CHUNK * AGES

    def cov_copy(n):
        rows = pl.ds(pl.multiple_of(n * span, 8), span)
        return pltpu.make_async_copy(flat.at[rows, :], cov_hbm.at[rows, :], cov_sem)

    def ages(n, _):
        for pair in range(CHUNK // 2):
            halves = []
            for h in range(2):
                i = n * CHUNK + pair * 2 + h
                block = jnp.transpose(outer[pl.ds(i, DB, stride=CROWS), :])
                block = block + jnp.where(sub == i, noise[pl.ds(i, 1), :], 0.0)
                halves.append(block[0:AGES, :])
            flat[pl.ds(pl.multiple_of(n * span + pair * 2 * AGES, 8), 2 * AGES), :] = jnp.concatenate(halves, axis=0)
        cov_copy(n).start()
        return 0
    lax.fori_loop(0, AGES // CHUNK, ages, 0)
    pltpu.make_async_copy(flat, cov_hbm, cov_sem).wait()
    out_marg.wait()


def blocks(slots):
    vmem = pl.BlockSpec(memory_space=pltpu.VMEM)
    hbm = pl.BlockSpec(memory_space=pltpu.MemorySpace.HBM)
    dma = pltpu.SemaphoreType.DMA
    marg, cov = pl.pallas_call(
        blocks_kernel,
        out_shape=(jax.ShapeDtypeStruct((DB, TABLE_TILES * LANES), jnp.float32),
                   jax.ShapeDtypeStruct((AGES * AGES, DB), jnp.float32)),
        in_specs=[vmem],
        out_specs=(hbm, hbm),
        scratch_shapes=[
            pltpu.VMEM((TABLE_TILES * DB, LANES), jnp.float32),
            pltpu.VMEM((DB, TABLE_TILES * LANES), jnp.float32),
            pltpu.VMEM((DB, LANES), jnp.float32),
            pltpu.VMEM((GROUP, LANES, LANES), jnp.float32),
            pltpu.VMEM((DB * CROWS, LANES), jnp.float32),
            pltpu.VMEM((AGES * AGES, DB), jnp.float32),
            dma(()), dma(()),
        ],
        compiler_params=pltpu.CompilerParams(vmem_limit_bytes=48 * 2**20),
        name="district_blocks",
    )(slots)
    return marg, cov.T


def shards(estimates, factors, variances, intersection_tracts, intersection_weights):
    keep = lambda a: pltpu.with_memory_space_constraint(a, pltpu.MemorySpace.HBM)
    slots = tile_sums(keep(intersection_tracts.T), keep(intersection_weights.T), keep(estimates), keep(factors), keep(variances))
    return blocks(slots)


def solution(mesh):
    return jax.shard_map(
        shards,
        mesh=mesh,
        in_specs=(
            P(("geo", "dist"), None),
            P(("geo", "dist"), None),
            P(("geo", "dist"), None),
            P("dist", None),
            P("dist", None),
        ),
        out_specs=(P("dist", None), P("dist", None)),
        check_vma=False,
    )
```

```python
import jax
import jax.numpy as jnp
from jax import lax
from jax.experimental import pallas as pl
from jax.experimental.pallas import tpu as pltpu
from jax.sharding import PartitionSpec as P

MESH = pl.DeviceIdType.MESH
GEO, DIST = 8, 16
DEVICES = GEO * DIST
LANES = 128
ROWS = 48
TRACTS = ROWS * DEVICES
BLOCK = ROWS * DIST
DB = 128
INTER = 32
TABLE_TILES = 58
HI, LO = TABLE_TILES, TABLE_TILES + 1
PER_X = 15
CHIPS = 4 * PER_X
HALF = DIST // 2
SLOTS = 2 * CHIPS
CODE_ROWS = DB + 8
STEPS = 32000.0
AGES, RANK = 116, 64
AHEAD = 3


GROUP = 8
CROWS = 120


def decode(slots, slot):
    code = slots[slot, 0:DB, :].astype(jnp.int32).astype(jnp.float32)
    e = slots[slot, DB:CODE_ROWS, :].astype(jnp.int32).astype(jnp.float32)
    return code * (jnp.exp2(e[0:1, :]) * (1.0 / STEPS))


def sums_kernel(idx_hbm, wgt_hbm, est_hbm, fac_hbm, var_hbm, out, outer,
                idx, wgt, est, fac, var, in_sem,
                pk, varp, table, weight, block, sums, coded,
                ready, own_sem, pk_send, pk_recv, row_send, row_recv, fwd_send, fwd_recv,
                tile_send, slot_recv, right_send, left_send, core_send, core_recv, loading, paired):
    g = lax.axis_index("geo")
    d = lax.axis_index("dist")
    me = g * DIST + d
    mine = d < PER_X
    x, c = lax.div(g, 2), lax.rem(g, 2)
    my_tile = x * PER_X + d
    at_home = lax.div(d, HALF) == c
    g_right = lax.rem(x + 1, 4) * 2 + c
    g_left = lax.rem(x + 3, 4) * 2 + c
    g_far = lax.rem(x + 2, 4) * 2 + c
    g_core = x * 2 + (1 - c)

    barrier = pltpu.get_barrier_semaphore()
    for s in range(1, DIST):
        pl.semaphore_signal(barrier, inc=1, device_id=(g, lax.rem(d + s, DIST)), device_id_type=MESH)
    for s in range(1, GEO):
        pl.semaphore_signal(barrier, inc=1, device_id=(lax.rem(g + s, GEO), d), device_id_type=MESH)

    loads = [pltpu.make_async_copy(src, dst, in_sem.at[n]) for n, (src, dst) in enumerate(
        ((idx_hbm, idx), (wgt_hbm, wgt), (var_hbm, var), (est_hbm, est), (fac_hbm, fac)))]
    for load in loads:
        load.start()

    loads[0].wait()
    loads[1].wait()
    pk[d] = idx[...] * 512 + wgt[...]
    varp[...] = jnp.zeros_like(varp)
    loads[2].wait()
    varp[:, 0:AGES] = var[...]
    loads[3].wait()
    loads[4].wait()

    my_range = pl.ds(pl.multiple_of(me * ROWS, 16), ROWS)
    sources = (fac, est)

    def for_tile(kind, t, also, action):
        @pl.when(jnp.logical_and(also, t < TABLE_TILES))
        def _():
            action(sources[kind].at[:, pl.ds(pl.multiple_of(t * LANES, LANES), LANES)])

        @pl.when(jnp.logical_and(also, t >= TABLE_TILES))
        def _():
            action(varp)

    for kind in range(2):
        for_tile(kind, my_tile, mine, lambda src: pltpu.make_async_copy(
            src, table.at[kind, my_range, :], row_recv.at[kind * 4 + x]).start())

    pl.semaphore_wait(barrier, DIST - 1 + GEO - 1)
    for s in range(1, GEO):
        pl.semaphore_signal(ready, inc=1, device_id=(lax.rem(g + s, GEO), d), device_id_type=MESH)

    def pk_copy(slot, to):
        return pltpu.make_async_remote_copy(
            src_ref=pk.at[slot], dst_ref=pk.at[slot], send_sem=pk_send.at[0],
            recv_sem=pk_recv.at[0], device_id=(g, to), device_id_type=MESH)

    @pl.when(at_home)
    def _():
        def pk_start(s, _):
            pk_copy(d, lax.rem(d + s, DIST)).start()
            return 0
        lax.fori_loop(1, DIST, pk_start, 0)

    def rows_to(kind, r):
        def one(k, _):
            de = lax.rem(d + k, DIST)
            xe = lax.rem(x + r + de, 4)
            other = jnp.logical_and(de < PER_X, jnp.logical_or(xe != x, de != d))
            for_tile(kind, xe * PER_X + de, other, lambda src: pltpu.make_async_remote_copy(
                src_ref=src, dst_ref=table.at[kind, my_range, :], send_sem=row_send.at[kind],
                recv_sem=row_recv.at[kind * 4 + x], device_id=(xe * 2 + c, de), device_id_type=MESH).start())
            return 0
        lax.fori_loop(0, DIST, one, 0)
    pl.semaphore_wait(ready, GEO - 1)
    for r in range(AHEAD):
        rows_to(0, r)

    def pk_wait(n, sem):
        ref = pk.at[pl.ds(0, n)]
        pltpu.make_async_copy(ref, ref, sem.at[0]).wait()

    @pl.when(at_home)
    def _():
        pk_wait(HALF - 1, pk_recv)

    @pl.when(jnp.logical_not(at_home))
    def _():
        pk_wait(HALF, pk_recv)
    lane = lax.broadcasted_iota(jnp.int32, (DB, LANES), 1)
    residue = lax.broadcasted_iota(jnp.int32, (64, DB), 0)

    def weights_of(n, _):
        entries = pk[c * HALF + n]
        res = lax.shift_right_logical(entries, 9) & 63
        val = (lax.shift_right_logical(entries, 15) * 512) + (entries & 511)
        acc = jnp.zeros((64, DB), jnp.int32)
        for k in range(INTER):
            acc = jnp.where(residue == res[k:k + 1, :], val[k:k + 1, :], acc)
        both = jnp.transpose(jnp.concatenate([acc, acc], axis=0))
        w = both & 511
        square = w * w
        w = jnp.where(my_tile == HI, lax.shift_right_logical(square, 8), jnp.where(my_tile == LO, square & 255, w))
        b = lax.shift_right_logical(both, 9) - jnp.where(lane >= 64, 1, 0)
        weight[n] = (w.astype(jnp.float32) * (1.0 / 256.0)).astype(jnp.bfloat16)
        block[n] = b.astype(jnp.float32).astype(jnp.bfloat16)
        return 0
    lax.fori_loop(0, HALF, weights_of, 0)

    many = 4

    def add_block(kind, gb):
        def part(q, _):
            w = weight[pl.ds(q * many, many)].reshape(many * DB, LANES)
            b = block[pl.ds(q * many, many)].reshape(many * DB, LANES)
            zero = jnp.zeros_like(w)
            total = None
            for step in range(BLOCK // 256):
                parts = []
                for h in range(2):
                    at = (2 * (gb * (BLOCK // LANES) + 2 * step + h)).astype(jnp.float32).astype(jnp.bfloat16)
                    parts.append(jnp.where(b == at, w, zero))
                rows = table[kind, pl.ds(pl.multiple_of(gb * BLOCK + step * 256, 256), 256), :]
                product = jnp.dot(jnp.concatenate(parts, axis=1), rows, preferred_element_type=jnp.float32)
                total = product if total is None else total + product
            sums[pl.ds(q * many, many)] += total.reshape(many, DB, LANES)
            return 0
        lax.fori_loop(0, HALF // many, part, 0)

    def block_rows(kind, gb):
        return table.at[kind, pl.ds(pl.multiple_of(gb * BLOCK, 256), BLOCK), :]

    def phase(kind, r, then):
        xs = lax.rem(x + 8 - lax.rem(d, 4) - r, 4)
        n = kind * 4 + xs
        own, other = xs * 2 + c, xs * 2 + 1 - c

        @pl.when(mine)
        def _():
            rows = block_rows(kind, own)
            pltpu.make_async_copy(rows, rows, row_recv.at[n]).wait()
            pltpu.make_async_remote_copy(
                src_ref=rows, dst_ref=rows, send_sem=fwd_send.at[kind], recv_sem=fwd_recv.at[n],
                device_id=(g_core, d), device_id_type=MESH).start()
        then()

        @pl.when(mine)
        def _():
            add_block(kind, own)
            rows = block_rows(kind, other)
            pltpu.make_async_copy(rows, rows, fwd_recv.at[n]).wait()
            add_block(kind, other)

    def side_of(kind, dd):
        return lax.rem(dd + kind, 2)

    def tile_copy(kind, n):
        slot = kind * CHIPS + my_tile
        return pltpu.make_async_remote_copy(
            src_ref=coded.at[kind, n], dst_ref=out.at[slot], send_sem=tile_send.at[kind], recv_sem=slot_recv.at[slot],
            device_id=(x * 2 + side_of(kind, d), c * HALF + n), device_id_type=MESH)

    def own_tile_copy(kind):
        return pltpu.make_async_copy(coded.at[kind, d - c * HALF], out.at[kind * CHIPS + my_tile], own_sem.at[kind])

    def stays(kind, dd):
        return jnp.logical_and(jnp.logical_and(dd == d, at_home), side_of(kind, d) == c)

    first = lax.rem(lax.div(d, many), 2)

    def encode(kind):
        def one(i, _):
            n = lax.rem(first + lax.div(i, many), 2) * many + lax.rem(d + i, many)
            total = sums[n]
            top = jnp.maximum(jnp.max(jnp.abs(total), axis=0, keepdims=True), 1e-30)
            e = jnp.ceil(jnp.log2(top))
            code = jnp.round(total * (STEPS / jnp.exp2(e)))
            coded[kind, n, 0:DB, :] = code.astype(jnp.int32).astype(jnp.int16)
            coded[kind, n, DB:CODE_ROWS, :] = jnp.broadcast_to(e, (8, LANES)).astype(jnp.int32).astype(jnp.int16)
            own = stays(kind, c * HALF + n)

            @pl.when(jnp.logical_not(own))
            def _():
                tile_copy(kind, n).start()

            @pl.when(own)
            def _():
                own_tile_copy(kind).start()
            return 0
        lax.fori_loop(0, HALF, one, 0)
        sums[...] = jnp.zeros_like(sums)

    def slot_copy(slot, send_sem, recv_sem, to_g):
        return pltpu.make_async_remote_copy(
            src_ref=out.at[slot], dst_ref=out.at[slot], send_sem=send_sem,
            recv_sem=recv_sem, device_id=(to_g, d), device_id_type=MESH)

    def arrived(slot):
        pltpu.make_async_copy(out.at[slot], out.at[slot], slot_recv.at[slot]).wait()

    def to_core(kind, slot):
        slot_copy(slot, core_send.at[0], core_recv.at[kind], g_core).start()

    def source(kind, j):
        i, m, b = lax.div(j, 4), lax.rem(lax.div(j, 2), 2), lax.rem(j, 2)
        k = 2 * m + lax.rem(d + c + kind, 2)
        return b * HALF + lax.rem(first + i, 2) * many + lax.rem(lax.rem(d, many) + many - k, many)

    def slot_at(kind, xx, dd):
        return kind * CHIPS + xx * PER_X + dd

    def from_dist(kind, j):
        dd = source(kind, j)
        slot = slot_at(kind, x, dd)

        @pl.when(dd < PER_X)
        def _():
            own = stays(kind, dd)

            @pl.when(own)
            def _():
                own_tile_copy(kind).wait()

            @pl.when(jnp.logical_not(own))
            def _():
                arrived(slot)
            slot_copy(slot, right_send.at[0], slot_recv.at[slot], g_right).start()
            slot_copy(slot, left_send.at[0], slot_recv.at[slot], g_left).start()
            to_core(kind, slot)

    def from_sides(kind, j):
        dd = source(kind, j)
        from_left = slot_at(kind, lax.rem(x + 3, 4), dd)
        from_right = slot_at(kind, lax.rem(x + 1, 4), dd)

        @pl.when(dd < PER_X)
        def _():
            arrived(from_left)

            @pl.when(lax.rem(lax.div(dd, 2), 2) == 0)
            def _():
                slot_copy(from_left, right_send.at[1], slot_recv.at[from_left], g_right).start()
            to_core(kind, from_left)
            arrived(from_right)

            @pl.when(lax.rem(lax.div(dd, 2), 2) == 1)
            def _():
                slot_copy(from_right, left_send.at[1], slot_recv.at[from_right], g_left).start()
            to_core(kind, from_right)

    def from_far(kind, j):
        dd = source(kind, j)

        @pl.when(dd < PER_X)
        def _():
            slot = slot_at(kind, lax.rem(x + 2, 4), dd)
            arrived(slot)
            to_core(kind, slot)

    def many_of(body, kind, start, stop):
        def one(j, _):
            body(kind, j)
            return 0
        lax.fori_loop(start, stop, one, 0)

    sums[...] = jnp.zeros_like(sums)
    for n in range(8):
        kind, r = n // 4, n % 4

        def then():
            if n + AHEAD < 8:
                rows_to((n + AHEAD) // 4, (n + AHEAD) % 4)
        phase(kind, r, then)
        if r == 3:
            @pl.when(mine)
            def _():
                encode(kind)
        if n == 5:
            many_of(from_dist, 0, 0, 4)
        if n == 6:
            many_of(from_dist, 0, 4, 8)
    many_of(from_sides, 0, 0, 8)
    many_of(from_dist, 1, 0, 4)
    many_of(from_far, 0, 0, 8)
    many_of(from_dist, 1, 4, 8)

    def wait_slots(sem, n):
        ref = out.at[pl.ds(0, n)]
        pltpu.make_async_copy(ref, ref, sem).wait()

    def from_core(kind):
        @pl.when(c == 1 - kind)
        def _():
            wait_slots(core_recv.at[kind], 4 * 8)

        @pl.when(c == kind)
        def _():
            wait_slots(core_recv.at[kind], 4 * 7)
    from_core(0)

    def load_tile(t, _):
        loading[pl.ds(pl.multiple_of(t * DB, DB), DB), :] = decode(out, t)
        return 0
    lax.fori_loop(0, TABLE_TILES, load_tile, 0)
    paired[...] = jnp.zeros_like(paired)
    low_row = lax.broadcasted_iota(jnp.int32, (TABLE_TILES, LANES), 1) < RANK
    low_full = lax.broadcasted_iota(jnp.int32, (LANES, LANES), 1) < RANK

    def group(grp, _):
        for k in range(GROUP):
            rows = loading[pl.ds(grp * GROUP + k, TABLE_TILES, stride=DB), :]
            turned = pltpu.roll(rows, RANK, axis=1)
            paired[k, pl.ds(0, TABLE_TILES, stride=2), :] = jnp.where(low_row, rows, turned)
            paired[k, pl.ds(1, TABLE_TILES, stride=2), :] = jnp.where(low_row, turned, rows)
        for k in range(GROUP):
            full = paired[k]
            hi = full.astype(jnp.bfloat16)
            lo = (full - hi.astype(jnp.float32)).astype(jnp.bfloat16)
            mixed = jnp.where(low_full, hi, lo)
            left = jnp.concatenate([mixed, mixed], axis=1)
            right = jnp.concatenate([hi, lo], axis=1)
            product = lax.dot_general(left, right, (((1,), (1,)), ((), ())), preferred_element_type=jnp.float32)
            outer[pl.ds(pl.multiple_of((grp * GROUP + k) * CROWS, 8), CROWS), :] = product[0:CROWS, :]

        @pl.when(grp < 8)
        def _():
            from_sides(1, grp)

        @pl.when(grp >= 8)
        def _():
            from_far(1, grp - 8)
        return 0
    lax.fori_loop(0, DB // GROUP, group, 0)

    from_core(1)
    wait_slots(core_send.at[0], 4 * PER_X)
    wait_slots(right_send.at[0], PER_X)
    wait_slots(left_send.at[0], PER_X)
    wait_slots(right_send.at[1], 8)
    wait_slots(left_send.at[1], 7)

    @pl.when(at_home)
    def _():
        pk_wait(DIST - 1, pk_send)

    for kind in range(2):
        def wait_rows(sem, n):
            ref = table.at[kind, pl.ds(0, n), :]
            pltpu.make_async_copy(ref, ref, sem.at[kind]).wait()

        @pl.when(mine)
        def _():
            wait_rows(row_send, (CHIPS - 1) * ROWS)
            wait_rows(fwd_send, 4 * BLOCK)
            own = stays(kind, d)

            @pl.when(own)
            def _():
                wait_slots(tile_send.at[kind], HALF - 1)

            @pl.when(jnp.logical_not(own))
            def _():
                wait_slots(tile_send.at[kind], HALF)

        @pl.when(jnp.logical_not(mine))
        def _():
            wait_rows(row_send, CHIPS * ROWS)


def tile_sums(idx, wgt, est, fac, var):
    vmem = pl.BlockSpec(memory_space=pltpu.VMEM)
    hbm = pl.BlockSpec(memory_space=pltpu.MemorySpace.HBM)
    dma = pltpu.SemaphoreType.DMA
    return pl.pallas_call(
        sums_kernel,
        out_shape=(jax.ShapeDtypeStruct((SLOTS, CODE_ROWS, LANES), jnp.int16),
                   jax.ShapeDtypeStruct((DB * CROWS, LANES), jnp.float32)),
        in_specs=[hbm] * 5,
        out_specs=(vmem, vmem),
        scratch_shapes=[
            pltpu.VMEM((INTER, DB), jnp.int32),
            pltpu.VMEM((INTER, DB), jnp.int32),
            pltpu.VMEM(est.shape, jnp.bfloat16),
            pltpu.VMEM(fac.shape, jnp.bfloat16),
            pltpu.VMEM(var.shape, jnp.bfloat16),
            dma((5,)),
            pltpu.VMEM((DIST, INTER, DB), jnp.int32),
            pltpu.VMEM((ROWS, LANES), jnp.bfloat16),
            pltpu.VMEM((2, TRACTS, LANES), jnp.bfloat16),
            pltpu.VMEM((HALF, DB, LANES), jnp.bfloat16),
            pltpu.VMEM((HALF, DB, LANES), jnp.bfloat16),
            pltpu.VMEM((HALF, DB, LANES), jnp.float32),
            pltpu.VMEM((2, HALF, CODE_ROWS, LANES), jnp.int16),
            pltpu.SemaphoreType.REGULAR, dma((2,)), dma((1,)), dma((1,)), dma((2,)), dma((8,)), dma((2,)), dma((8,)),
            dma((2,)), dma((SLOTS,)), dma((2,)), dma((2,)), dma((1,)), dma((2,)),
            pltpu.VMEM((TABLE_TILES * DB, LANES), jnp.float32),
            pltpu.VMEM((GROUP, LANES, LANES), jnp.float32),
        ],
        compiler_params=pltpu.CompilerParams(has_side_effects=True, collective_id=0, vmem_limit_bytes=32 * 2**20),
        name="tile_sums",
    )(idx, wgt, est, fac, var)


CHUNK = 4


def blocks_kernel(slots, outer, marg_hbm, cov_hbm, marg, noise, flat, marg_sem, cov_sem):
    noise[...] = jnp.transpose(decode(slots, HI) + decode(slots, LO) * (1.0 / 256.0))
    sub = lax.broadcasted_iota(jnp.int32, (LANES, LANES), 0)

    span = CHUNK * AGES

    def cov_copy(n):
        rows = pl.ds(pl.multiple_of(n * span, 8), span)
        return pltpu.make_async_copy(flat.at[rows, :], cov_hbm.at[rows, :], cov_sem)

    def ages(n, _):
        for pair in range(CHUNK // 2):
            halves = []
            for h in range(2):
                i = n * CHUNK + pair * 2 + h
                block = jnp.transpose(outer[pl.ds(i, DB, stride=CROWS), :])
                block = block + jnp.where(sub == i, noise[pl.ds(i, 1), :], 0.0)
                halves.append(block[0:AGES, :])
            flat[pl.ds(pl.multiple_of(n * span + pair * 2 * AGES, 8), 2 * AGES), :] = jnp.concatenate(halves, axis=0)
        cov_copy(n).start()
        return 0
    lax.fori_loop(0, AGES // CHUNK, ages, 0)
    for t in range(TABLE_TILES):
        marg[:, t * LANES:(t + 1) * LANES] = decode(slots, CHIPS + t)
    out_marg = pltpu.make_async_copy(marg, marg_hbm, marg_sem)
    out_marg.start()
    pltpu.make_async_copy(flat, cov_hbm, cov_sem).wait()
    out_marg.wait()


def blocks(slots, outer):
    vmem = pl.BlockSpec(memory_space=pltpu.VMEM)
    hbm = pl.BlockSpec(memory_space=pltpu.MemorySpace.HBM)
    dma = pltpu.SemaphoreType.DMA
    marg, cov = pl.pallas_call(
        blocks_kernel,
        out_shape=(jax.ShapeDtypeStruct((DB, TABLE_TILES * LANES), jnp.float32),
                   jax.ShapeDtypeStruct((AGES * AGES, DB), jnp.float32)),
        in_specs=[vmem, vmem],
        out_specs=(hbm, hbm),
        scratch_shapes=[
            pltpu.VMEM((DB, TABLE_TILES * LANES), jnp.float32),
            pltpu.VMEM((DB, LANES), jnp.float32),
            pltpu.VMEM((AGES * AGES, DB), jnp.float32),
            dma(()), dma(()),
        ],
        compiler_params=pltpu.CompilerParams(vmem_limit_bytes=24 * 2**20),
        name="district_blocks",
    )(slots, outer)
    return marg, cov.T


def shards(estimates, factors, variances, intersection_tracts, intersection_weights):
    keep = lambda a: pltpu.with_memory_space_constraint(a, pltpu.MemorySpace.HBM)
    slots, outer = tile_sums(keep(intersection_tracts.T), keep(intersection_weights.T), keep(estimates), keep(factors), keep(variances))
    return blocks(slots, outer)


def solution(mesh):
    return jax.shard_map(
        shards,
        mesh=mesh,
        in_specs=(
            P(("geo", "dist"), None),
            P(("geo", "dist"), None),
            P(("geo", "dist"), None),
            P("dist", None),
            P("dist", None),
        ),
        out_specs=(P("dist", None), P("dist", None)),
        check_vma=False,
    )
```

```python
import jax
import jax.numpy as jnp
from jax import lax
from jax.experimental import pallas as pl
from jax.experimental.pallas import tpu as pltpu
from jax.sharding import PartitionSpec as P

MESH = pl.DeviceIdType.MESH
GEO, DIST = 8, 16
DEVICES = GEO * DIST
LANES = 128
ROWS = 48
TRACTS = ROWS * DEVICES
BLOCK = ROWS * DIST
DB = 128
INTER = 32
TABLE_TILES = 58
HI, LO = TABLE_TILES, TABLE_TILES + 1
PER_X = 15
CHIPS = 4 * PER_X
HALF = DIST // 2
SLOTS = 2 * CHIPS
CODE_ROWS = DB + 8
STEPS = 32000.0
AGES, RANK = 116, 64
AHEAD = 3


GROUP = 8
CROWS = 120
SPREAD = DB + 8


def decode(slots, slot):
    code = slots[slot, 0:DB, :].astype(jnp.int32).astype(jnp.float32)
    e = slots[slot, DB:CODE_ROWS, :].astype(jnp.int32).astype(jnp.float32)
    return code * (jnp.exp2(e[0:1, :]) * (1.0 / STEPS))


def sums_kernel(idx_hbm, wgt_hbm, est_hbm, fac_hbm, var_hbm, out, outer,
                idx, wgt, est, fac, var, in_sem,
                pk, varp, table, weight, block, sums, coded,
                ready, own_sem, pk_send, pk_recv, row_send, row_recv, fwd_send, fwd_recv,
                tile_send, slot_recv, right_send, left_send, core_send, core_recv, loading, paired):
    g = lax.axis_index("geo")
    d = lax.axis_index("dist")
    me = g * DIST + d
    mine = d < PER_X
    x, c = lax.div(g, 2), lax.rem(g, 2)
    my_tile = x * PER_X + d
    at_home = lax.div(d, HALF) == c
    g_right = lax.rem(x + 1, 4) * 2 + c
    g_left = lax.rem(x + 3, 4) * 2 + c
    g_far = lax.rem(x + 2, 4) * 2 + c
    g_core = x * 2 + (1 - c)

    barrier = pltpu.get_barrier_semaphore()
    for s in range(1, DIST):
        pl.semaphore_signal(barrier, inc=1, device_id=(g, lax.rem(d + s, DIST)), device_id_type=MESH)
    for s in range(1, GEO):
        pl.semaphore_signal(barrier, inc=1, device_id=(lax.rem(g + s, GEO), d), device_id_type=MESH)

    loads = [pltpu.make_async_copy(src, dst, in_sem.at[n]) for n, (src, dst) in enumerate(
        ((idx_hbm, idx), (wgt_hbm, wgt), (var_hbm, var), (est_hbm, est), (fac_hbm, fac)))]
    for load in loads:
        load.start()

    loads[0].wait()
    loads[1].wait()
    pk[d] = idx[...] * 512 + wgt[...]
    varp[...] = jnp.zeros_like(varp)
    loads[2].wait()
    varp[:, 0:AGES] = var[...]
    loads[3].wait()
    loads[4].wait()

    my_range = pl.ds(pl.multiple_of(me * ROWS, 16), ROWS)
    sources = (fac, est)

    def for_tile(kind, t, also, action):
        @pl.when(jnp.logical_and(also, t < TABLE_TILES))
        def _():
            action(sources[kind].at[:, pl.ds(pl.multiple_of(t * LANES, LANES), LANES)])

        @pl.when(jnp.logical_and(also, t >= TABLE_TILES))
        def _():
            action(varp)

    for kind in range(2):
        for_tile(kind, my_tile, mine, lambda src: pltpu.make_async_copy(
            src, table.at[kind, my_range, :], row_recv.at[kind * 4 + x]).start())

    pl.semaphore_wait(barrier, DIST - 1 + GEO - 1)
    for s in range(1, GEO):
        pl.semaphore_signal(ready, inc=1, device_id=(lax.rem(g + s, GEO), d), device_id_type=MESH)

    def pk_copy(slot, to):
        return pltpu.make_async_remote_copy(
            src_ref=pk.at[slot], dst_ref=pk.at[slot], send_sem=pk_send.at[0],
            recv_sem=pk_recv.at[0], device_id=(g, to), device_id_type=MESH)

    @pl.when(at_home)
    def _():
        def pk_start(s, _):
            pk_copy(d, lax.rem(d + s, DIST)).start()
            return 0
        lax.fori_loop(1, DIST, pk_start, 0)

    def rows_to(kind, r):
        def one(k, _):
            de = lax.rem(d + k, DIST)
            xe = lax.rem(x + r + de, 4)
            other = jnp.logical_and(de < PER_X, jnp.logical_or(xe != x, de != d))
            for_tile(kind, xe * PER_X + de, other, lambda src: pltpu.make_async_remote_copy(
                src_ref=src, dst_ref=table.at[kind, my_range, :], send_sem=row_send.at[kind],
                recv_sem=row_recv.at[kind * 4 + x], device_id=(xe * 2 + c, de), device_id_type=MESH).start())
            return 0
        lax.fori_loop(0, DIST, one, 0)
    pl.semaphore_wait(ready, GEO - 1)
    for r in range(AHEAD):
        rows_to(0, r)

    def pk_wait(n, sem):
        ref = pk.at[pl.ds(0, n)]
        pltpu.make_async_copy(ref, ref, sem.at[0]).wait()

    @pl.when(at_home)
    def _():
        pk_wait(HALF - 1, pk_recv)

    @pl.when(jnp.logical_not(at_home))
    def _():
        pk_wait(HALF, pk_recv)
    lane = lax.broadcasted_iota(jnp.int32, (DB, LANES), 1)
    residue = lax.broadcasted_iota(jnp.int32, (64, DB), 0)

    def weights_of(n, _):
        entries = pk[c * HALF + n]
        res = lax.shift_right_logical(entries, 9) & 63
        val = (lax.shift_right_logical(entries, 15) * 512) + (entries & 511)
        acc = jnp.zeros((64, DB), jnp.int32)
        for k in range(INTER):
            acc = jnp.where(residue == res[k:k + 1, :], val[k:k + 1, :], acc)
        both = jnp.transpose(jnp.concatenate([acc, acc], axis=0))
        w = both & 511
        square = w * w
        w = jnp.where(my_tile == HI, lax.shift_right_logical(square, 8), jnp.where(my_tile == LO, square & 255, w))
        b = lax.shift_right_logical(both, 9) - jnp.where(lane >= 64, 1, 0)
        weight[n] = (w.astype(jnp.float32) * (1.0 / 256.0)).astype(jnp.bfloat16)
        block[n] = b.astype(jnp.float32).astype(jnp.bfloat16)
        return 0
    lax.fori_loop(0, HALF, weights_of, 0)

    many = 4

    def add_block(kind, gb):
        def part(q, _):
            w = weight[pl.ds(q * many, many)].reshape(many * DB, LANES)
            b = block[pl.ds(q * many, many)].reshape(many * DB, LANES)
            zero = jnp.zeros_like(w)
            total = None
            for step in range(BLOCK // 256):
                parts = []
                for h in range(2):
                    at = (2 * (gb * (BLOCK // LANES) + 2 * step + h)).astype(jnp.float32).astype(jnp.bfloat16)
                    parts.append(jnp.where(b == at, w, zero))
                rows = table[kind, pl.ds(pl.multiple_of(gb * BLOCK + step * 256, 256), 256), :]
                product = jnp.dot(jnp.concatenate(parts, axis=1), rows, preferred_element_type=jnp.float32)
                total = product if total is None else total + product
            sums[pl.ds(q * many, many)] += total.reshape(many, DB, LANES)
            return 0
        lax.fori_loop(0, HALF // many, part, 0)

    def block_rows(kind, gb):
        return table.at[kind, pl.ds(pl.multiple_of(gb * BLOCK, 256), BLOCK), :]

    def phase(kind, r, then):
        xs = lax.rem(x + 8 - lax.rem(d, 4) - r, 4)
        n = kind * 4 + xs
        own, other = xs * 2 + c, xs * 2 + 1 - c

        @pl.when(mine)
        def _():
            rows = block_rows(kind, own)
            pltpu.make_async_copy(rows, rows, row_recv.at[n]).wait()
            pltpu.make_async_remote_copy(
                src_ref=rows, dst_ref=rows, send_sem=fwd_send.at[kind], recv_sem=fwd_recv.at[n],
                device_id=(g_core, d), device_id_type=MESH).start()
        then()

        @pl.when(mine)
        def _():
            add_block(kind, own)
            rows = block_rows(kind, other)
            pltpu.make_async_copy(rows, rows, fwd_recv.at[n]).wait()
            add_block(kind, other)

    def side_of(kind, dd):
        return lax.rem(dd + kind, 2)

    def tile_copy(kind, n):
        slot = kind * CHIPS + my_tile
        return pltpu.make_async_remote_copy(
            src_ref=coded.at[kind, n], dst_ref=out.at[slot], send_sem=tile_send.at[kind], recv_sem=slot_recv.at[slot],
            device_id=(x * 2 + side_of(kind, d), c * HALF + n), device_id_type=MESH)

    def own_tile_copy(kind):
        return pltpu.make_async_copy(coded.at[kind, d - c * HALF], out.at[kind * CHIPS + my_tile], own_sem.at[kind])

    def stays(kind, dd):
        return jnp.logical_and(jnp.logical_and(dd == d, at_home), side_of(kind, d) == c)

    first = lax.rem(lax.div(d, many), 2)

    def encode(kind):
        def one(i, _):
            n = lax.rem(first + lax.div(i, many), 2) * many + lax.rem(d + i, many)
            total = sums[n]
            top = jnp.maximum(jnp.max(jnp.abs(total), axis=0, keepdims=True), 1e-30)
            e = jnp.ceil(jnp.log2(top))
            code = jnp.round(total * (STEPS / jnp.exp2(e)))
            coded[kind, n, 0:DB, :] = code.astype(jnp.int32).astype(jnp.int16)
            coded[kind, n, DB:CODE_ROWS, :] = jnp.broadcast_to(e, (8, LANES)).astype(jnp.int32).astype(jnp.int16)
            own = stays(kind, c * HALF + n)

            @pl.when(jnp.logical_not(own))
            def _():
                tile_copy(kind, n).start()

            @pl.when(own)
            def _():
                own_tile_copy(kind).start()
            return 0
        lax.fori_loop(0, HALF, one, 0)
        sums[...] = jnp.zeros_like(sums)

    def slot_copy(slot, send_sem, recv_sem, to_g):
        return pltpu.make_async_remote_copy(
            src_ref=out.at[slot], dst_ref=out.at[slot], send_sem=send_sem,
            recv_sem=recv_sem, device_id=(to_g, d), device_id_type=MESH)

    def arrived(slot):
        pltpu.make_async_copy(out.at[slot], out.at[slot], slot_recv.at[slot]).wait()

    def to_core(kind, slot):
        slot_copy(slot, core_send.at[0], core_recv.at[kind], g_core).start()

    def source(kind, j):
        i, m, b = lax.div(j, 4), lax.rem(lax.div(j, 2), 2), lax.rem(j, 2)
        k = 2 * m + lax.rem(d + c + kind, 2)
        return b * HALF + lax.rem(first + i, 2) * many + lax.rem(lax.rem(d, many) + many - k, many)

    def slot_at(kind, xx, dd):
        return kind * CHIPS + xx * PER_X + dd

    def from_dist(kind, j):
        dd = source(kind, j)
        slot = slot_at(kind, x, dd)

        @pl.when(dd < PER_X)
        def _():
            own = stays(kind, dd)

            @pl.when(own)
            def _():
                own_tile_copy(kind).wait()

            @pl.when(jnp.logical_not(own))
            def _():
                arrived(slot)
            slot_copy(slot, right_send.at[0], slot_recv.at[slot], g_right).start()
            slot_copy(slot, left_send.at[0], slot_recv.at[slot], g_left).start()
            to_core(kind, slot)

    def from_sides(kind, j):
        dd = source(kind, j)
        from_left = slot_at(kind, lax.rem(x + 3, 4), dd)
        from_right = slot_at(kind, lax.rem(x + 1, 4), dd)

        @pl.when(dd < PER_X)
        def _():
            arrived(from_left)

            @pl.when(lax.rem(lax.div(dd, 2), 2) == 0)
            def _():
                slot_copy(from_left, right_send.at[1], slot_recv.at[from_left], g_right).start()
            to_core(kind, from_left)
            arrived(from_right)

            @pl.when(lax.rem(lax.div(dd, 2), 2) == 1)
            def _():
                slot_copy(from_right, left_send.at[1], slot_recv.at[from_right], g_left).start()
            to_core(kind, from_right)

    def from_far(kind, j):
        dd = source(kind, j)

        @pl.when(dd < PER_X)
        def _():
            slot = slot_at(kind, lax.rem(x + 2, 4), dd)
            arrived(slot)
            to_core(kind, slot)

    def many_of(body, kind, start, stop):
        def one(j, _):
            body(kind, j)
            return 0
        lax.fori_loop(start, stop, one, 0)

    sums[...] = jnp.zeros_like(sums)
    for n in range(8):
        kind, r = n // 4, n % 4

        def then():
            if n + AHEAD < 8:
                rows_to((n + AHEAD) // 4, (n + AHEAD) % 4)
        phase(kind, r, then)
        if r == 3:
            @pl.when(mine)
            def _():
                encode(kind)
        if n == 5:
            many_of(from_dist, 0, 0, 4)
        if n == 6:
            many_of(from_dist, 0, 4, 8)
    many_of(from_sides, 0, 0, 8)
    many_of(from_dist, 1, 0, 4)
    many_of(from_far, 0, 0, 8)
    many_of(from_dist, 1, 4, 8)

    def wait_slots(sem, n):
        ref = out.at[pl.ds(0, n)]
        pltpu.make_async_copy(ref, ref, sem).wait()

    def from_core(kind):
        @pl.when(c == 1 - kind)
        def _():
            wait_slots(core_recv.at[kind], 4 * 8)

        @pl.when(c == kind)
        def _():
            wait_slots(core_recv.at[kind], 4 * 7)
    from_core(0)

    def load_tile(t, _):
        loading[pl.ds(pl.multiple_of(t * SPREAD, 8), DB), :] = decode(out, t)
        return 0
    lax.fori_loop(0, TABLE_TILES, load_tile, 0)
    paired[...] = jnp.zeros_like(paired)
    low_row = lax.broadcasted_iota(jnp.int32, (TABLE_TILES, LANES), 1) < RANK
    low_full = lax.broadcasted_iota(jnp.int32, (LANES, LANES), 1) < RANK

    def group(grp, _):
        for k in range(GROUP):
            rows = loading[pl.ds(grp * GROUP + k, TABLE_TILES, stride=SPREAD), :]
            turned = pltpu.roll(rows, RANK, axis=1)
            paired[k, pl.ds(0, TABLE_TILES, stride=2), :] = jnp.where(low_row, rows, turned)
            paired[k, pl.ds(1, TABLE_TILES, stride=2), :] = jnp.where(low_row, turned, rows)
        for k in range(GROUP):
            full = paired[k]
            hi = full.astype(jnp.bfloat16)
            lo = (full - hi.astype(jnp.float32)).astype(jnp.bfloat16)
            mixed = jnp.where(low_full, hi, lo)
            left = jnp.concatenate([mixed, mixed], axis=1)
            right = jnp.concatenate([hi, lo], axis=1)
            product = lax.dot_general(left, right, (((1,), (1,)), ((), ())), preferred_element_type=jnp.float32)
            outer[pl.ds(pl.multiple_of((grp * GROUP + k) * CROWS, 8), CROWS), :] = product[0:CROWS, :]

        @pl.when(grp < 8)
        def _():
            from_sides(1, grp)

        @pl.when(grp >= 8)
        def _():
            from_far(1, grp - 8)
        return 0
    lax.fori_loop(0, DB // GROUP, group, 0)

    from_core(1)
    wait_slots(core_send.at[0], 4 * PER_X)
    wait_slots(right_send.at[0], PER_X)
    wait_slots(left_send.at[0], PER_X)
    wait_slots(right_send.at[1], 8)
    wait_slots(left_send.at[1], 7)

    @pl.when(at_home)
    def _():
        pk_wait(DIST - 1, pk_send)

    for kind in range(2):
        def wait_rows(sem, n):
            ref = table.at[kind, pl.ds(0, n), :]
            pltpu.make_async_copy(ref, ref, sem.at[kind]).wait()

        @pl.when(mine)
        def _():
            wait_rows(row_send, (CHIPS - 1) * ROWS)
            wait_rows(fwd_send, 4 * BLOCK)
            own = stays(kind, d)

            @pl.when(own)
            def _():
                wait_slots(tile_send.at[kind], HALF - 1)

            @pl.when(jnp.logical_not(own))
            def _():
                wait_slots(tile_send.at[kind], HALF)

        @pl.when(jnp.logical_not(mine))
        def _():
            wait_rows(row_send, CHIPS * ROWS)


def tile_sums(idx, wgt, est, fac, var):
    vmem = pl.BlockSpec(memory_space=pltpu.VMEM)
    hbm = pl.BlockSpec(memory_space=pltpu.MemorySpace.HBM)
    dma = pltpu.SemaphoreType.DMA
    return pl.pallas_call(
        sums_kernel,
        out_shape=(jax.ShapeDtypeStruct((SLOTS, CODE_ROWS, LANES), jnp.int16),
                   jax.ShapeDtypeStruct((DB * CROWS, LANES), jnp.float32)),
        in_specs=[hbm] * 5,
        out_specs=(vmem, vmem),
        scratch_shapes=[
            pltpu.VMEM((INTER, DB), jnp.int32),
            pltpu.VMEM((INTER, DB), jnp.int32),
            pltpu.VMEM(est.shape, jnp.bfloat16),
            pltpu.VMEM(fac.shape, jnp.bfloat16),
            pltpu.VMEM(var.shape, jnp.bfloat16),
            dma((5,)),
            pltpu.VMEM((DIST, INTER, DB), jnp.int32),
            pltpu.VMEM((ROWS, LANES), jnp.bfloat16),
            pltpu.VMEM((2, TRACTS, LANES), jnp.bfloat16),
            pltpu.VMEM((HALF, DB, LANES), jnp.bfloat16),
            pltpu.VMEM((HALF, DB, LANES), jnp.bfloat16),
            pltpu.VMEM((HALF, DB, LANES), jnp.float32),
            pltpu.VMEM((2, HALF, CODE_ROWS, LANES), jnp.int16),
            pltpu.SemaphoreType.REGULAR, dma((2,)), dma((1,)), dma((1,)), dma((2,)), dma((8,)), dma((2,)), dma((8,)),
            dma((2,)), dma((SLOTS,)), dma((2,)), dma((2,)), dma((1,)), dma((2,)),
            pltpu.VMEM((TABLE_TILES * SPREAD, LANES), jnp.float32),
            pltpu.VMEM((GROUP, LANES, LANES), jnp.float32),
        ],
        compiler_params=pltpu.CompilerParams(has_side_effects=True, collective_id=0, vmem_limit_bytes=32 * 2**20),
        name="tile_sums",
    )(idx, wgt, est, fac, var)


CHUNK = 4


def blocks_kernel(slots, outer, marg_hbm, cov_hbm, marg, noise, flat, marg_sem, cov_sem):
    noise[...] = jnp.transpose(decode(slots, HI) + decode(slots, LO) * (1.0 / 256.0))
    sub = lax.broadcasted_iota(jnp.int32, (LANES, LANES), 0)

    span = CHUNK * AGES

    def cov_copy(n):
        rows = pl.ds(pl.multiple_of(n * span, 8), span)
        return pltpu.make_async_copy(flat.at[rows, :], cov_hbm.at[rows, :], cov_sem)

    def ages(n, _):
        for pair in range(CHUNK // 2):
            halves = []
            for h in range(2):
                i = n * CHUNK + pair * 2 + h
                block = jnp.transpose(outer[pl.ds(i, DB, stride=CROWS), :])
                block = block + jnp.where(sub == i, noise[pl.ds(i, 1), :], 0.0)
                halves.append(block[0:AGES, :])
            flat[pl.ds(pl.multiple_of(n * span + pair * 2 * AGES, 8), 2 * AGES), :] = jnp.concatenate(halves, axis=0)
        cov_copy(n).start()
        return 0
    lax.fori_loop(0, AGES // CHUNK, ages, 0)
    for t in range(TABLE_TILES):
        marg[:, t * LANES:(t + 1) * LANES] = decode(slots, CHIPS + t)
    out_marg = pltpu.make_async_copy(marg, marg_hbm, marg_sem)
    out_marg.start()
    pltpu.make_async_copy(flat, cov_hbm, cov_sem).wait()
    out_marg.wait()


def blocks(slots, outer):
    vmem = pl.BlockSpec(memory_space=pltpu.VMEM)
    hbm = pl.BlockSpec(memory_space=pltpu.MemorySpace.HBM)
    dma = pltpu.SemaphoreType.DMA
    marg, cov = pl.pallas_call(
        blocks_kernel,
        out_shape=(jax.ShapeDtypeStruct((DB, TABLE_TILES * LANES), jnp.float32),
                   jax.ShapeDtypeStruct((AGES * AGES, DB), jnp.float32)),
        in_specs=[vmem, vmem],
        out_specs=(hbm, hbm),
        scratch_shapes=[
            pltpu.VMEM((DB, TABLE_TILES * LANES), jnp.float32),
            pltpu.VMEM((DB, LANES), jnp.float32),
            pltpu.VMEM((AGES * AGES, DB), jnp.float32),
            dma(()), dma(()),
        ],
        compiler_params=pltpu.CompilerParams(vmem_limit_bytes=24 * 2**20),
        name="district_blocks",
    )(slots, outer)
    return marg, cov.T


def shards(estimates, factors, variances, intersection_tracts, intersection_weights):
    keep = lambda a: pltpu.with_memory_space_constraint(a, pltpu.MemorySpace.HBM)
    slots, outer = tile_sums(keep(intersection_tracts.T), keep(intersection_weights.T), keep(estimates), keep(factors), keep(variances))
    return blocks(slots, outer)


def solution(mesh):
    return jax.shard_map(
        shards,
        mesh=mesh,
        in_specs=(
            P(("geo", "dist"), None),
            P(("geo", "dist"), None),
            P(("geo", "dist"), None),
            P("dist", None),
            P("dist", None),
        ),
        out_specs=(P("dist", None), P("dist", None)),
        check_vma=False,
    )
```

```python
import jax
import jax.numpy as jnp
from jax import lax
from jax.experimental import pallas as pl
from jax.experimental.pallas import tpu as pltpu
from jax.sharding import PartitionSpec as P

MESH = pl.DeviceIdType.MESH
GEO, DIST = 8, 16
DEVICES = GEO * DIST
LANES = 128
ROWS = 48
TRACTS = ROWS * DEVICES
BLOCK = ROWS * DIST
DB = 128
INTER = 32
TABLE_TILES = 58
HI, LO = TABLE_TILES, TABLE_TILES + 1
PER_X = 15
CHIPS = 4 * PER_X
HALF = DIST // 2
SLOTS = 2 * CHIPS
CODE_ROWS = DB + 8
STEPS = 32000.0
AGES, RANK = 116, 64
AHEAD = 3


GROUP = 8
CROWS = 120
SPREAD = DB + 8


def decode(slots, slot):
    code = slots[slot, 0:DB, :].astype(jnp.int32).astype(jnp.float32)
    e = slots[slot, DB:CODE_ROWS, :].astype(jnp.int32).astype(jnp.float32)
    return code * (jnp.exp2(e[0:1, :]) * (1.0 / STEPS))


def sums_kernel(idx_hbm, wgt_hbm, est_hbm, fac_hbm, var_hbm, out, outer,
                idx, wgt, est, fac, var, in_sem,
                pk, varp, table, weight, block, sums, coded,
                ready, own_sem, pk_send, pk_recv, row_send, row_recv, fwd_send, fwd_recv,
                tile_send, slot_recv, right_send, left_send, core_send, core_recv, loading, paired):
    g = lax.axis_index("geo")
    d = lax.axis_index("dist")
    me = g * DIST + d
    mine = d < PER_X
    x, c = lax.div(g, 2), lax.rem(g, 2)
    my_tile = x * PER_X + d
    at_home = lax.div(d, HALF) == c
    g_right = lax.rem(x + 1, 4) * 2 + c
    g_left = lax.rem(x + 3, 4) * 2 + c
    g_far = lax.rem(x + 2, 4) * 2 + c
    g_core = x * 2 + (1 - c)

    barrier = pltpu.get_barrier_semaphore()
    for s in range(1, DIST):
        pl.semaphore_signal(barrier, inc=1, device_id=(g, lax.rem(d + s, DIST)), device_id_type=MESH)
    for s in range(1, GEO):
        pl.semaphore_signal(barrier, inc=1, device_id=(lax.rem(g + s, GEO), d), device_id_type=MESH)

    loads = [pltpu.make_async_copy(src, dst, in_sem.at[n]) for n, (src, dst) in enumerate(
        ((idx_hbm, idx), (wgt_hbm, wgt), (var_hbm, var), (est_hbm, est), (fac_hbm, fac)))]
    for load in loads:
        load.start()

    loads[0].wait()
    loads[1].wait()
    pk[d] = idx[...] * 512 + wgt[...]
    varp[...] = jnp.zeros_like(varp)
    loads[2].wait()
    varp[:, 0:AGES] = var[...]
    loads[3].wait()
    loads[4].wait()

    my_range = pl.ds(pl.multiple_of(me * ROWS, 16), ROWS)
    sources = (fac, est)

    def for_tile(kind, t, also, action):
        @pl.when(jnp.logical_and(also, t < TABLE_TILES))
        def _():
            action(sources[kind].at[:, pl.ds(pl.multiple_of(t * LANES, LANES), LANES)])

        @pl.when(jnp.logical_and(also, t >= TABLE_TILES))
        def _():
            action(varp)

    for kind in range(2):
        for_tile(kind, my_tile, mine, lambda src: pltpu.make_async_copy(
            src, table.at[kind, my_range, :], row_recv.at[kind * 4 + x]).start())

    pl.semaphore_wait(barrier, DIST - 1 + GEO - 1)
    for s in range(1, GEO):
        pl.semaphore_signal(ready, inc=1, device_id=(lax.rem(g + s, GEO), d), device_id_type=MESH)

    def pk_copy(slot, to):
        return pltpu.make_async_remote_copy(
            src_ref=pk.at[slot], dst_ref=pk.at[slot], send_sem=pk_send.at[0],
            recv_sem=pk_recv.at[0], device_id=(g, to), device_id_type=MESH)

    @pl.when(at_home)
    def _():
        def pk_start(s, _):
            pk_copy(d, lax.rem(d + s, DIST)).start()
            return 0
        lax.fori_loop(1, DIST, pk_start, 0)

    def rows_to(kind, r):
        def one(k, _):
            de = lax.rem(d + k, DIST)
            xe = lax.rem(x + r + de, 4)
            other = jnp.logical_and(de < PER_X, jnp.logical_or(xe != x, de != d))
            for_tile(kind, xe * PER_X + de, other, lambda src: pltpu.make_async_remote_copy(
                src_ref=src, dst_ref=table.at[kind, my_range, :], send_sem=row_send.at[kind],
                recv_sem=row_recv.at[kind * 4 + x], device_id=(xe * 2 + c, de), device_id_type=MESH).start())
            return 0
        lax.fori_loop(0, DIST, one, 0)
    pl.semaphore_wait(ready, GEO - 1)
    for r in range(AHEAD):
        rows_to(0, r)

    def pk_wait(n, sem):
        ref = pk.at[pl.ds(0, n)]
        pltpu.make_async_copy(ref, ref, sem.at[0]).wait()

    @pl.when(at_home)
    def _():
        pk_wait(HALF - 1, pk_recv)

    @pl.when(jnp.logical_not(at_home))
    def _():
        pk_wait(HALF, pk_recv)
    lane = lax.broadcasted_iota(jnp.int32, (DB, LANES), 1)
    residue = lax.broadcasted_iota(jnp.int32, (64, DB), 0)

    def weights_of(n, _):
        entries = pk[c * HALF + n]
        res = lax.shift_right_logical(entries, 9) & 63
        val = (lax.shift_right_logical(entries, 15) * 512) + (entries & 511)
        acc = jnp.zeros((64, DB), jnp.int32)
        for k in range(INTER):
            acc = jnp.where(residue == res[k:k + 1, :], val[k:k + 1, :], acc)
        both = jnp.transpose(jnp.concatenate([acc, acc], axis=0))
        w = both & 511
        square = w * w
        w = jnp.where(my_tile == HI, lax.shift_right_logical(square, 8), jnp.where(my_tile == LO, square & 255, w))
        b = lax.shift_right_logical(both, 9) - jnp.where(lane >= 64, 1, 0)
        weight[n] = (w.astype(jnp.float32) * (1.0 / 256.0)).astype(jnp.bfloat16)
        block[n] = b.astype(jnp.float32).astype(jnp.bfloat16)
        return 0
    lax.fori_loop(0, HALF, weights_of, 0)

    many = 4

    def add_block(kind, gb):
        def part(q, _):
            w = weight[pl.ds(q * many, many)].reshape(many * DB, LANES)
            b = block[pl.ds(q * many, many)].reshape(many * DB, LANES)
            zero = jnp.zeros_like(w)
            total = None
            for step in range(BLOCK // 256):
                parts = []
                for h in range(2):
                    at = (2 * (gb * (BLOCK // LANES) + 2 * step + h)).astype(jnp.float32).astype(jnp.bfloat16)
                    parts.append(jnp.where(b == at, w, zero))
                rows = table[kind, pl.ds(pl.multiple_of(gb * BLOCK + step * 256, 256), 256), :]
                product = jnp.dot(jnp.concatenate(parts, axis=1), rows, preferred_element_type=jnp.float32)
                total = product if total is None else total + product
            sums[pl.ds(q * many, many)] += total.reshape(many, DB, LANES)
            return 0
        lax.fori_loop(0, HALF // many, part, 0)

    def block_rows(kind, gb):
        return table.at[kind, pl.ds(pl.multiple_of(gb * BLOCK, 256), BLOCK), :]

    def phase(kind, r, then):
        xs = lax.rem(x + 8 - lax.rem(d, 4) - r, 4)
        n = kind * 4 + xs
        own, other = xs * 2 + c, xs * 2 + 1 - c

        @pl.when(mine)
        def _():
            rows = block_rows(kind, own)
            pltpu.make_async_copy(rows, rows, row_recv.at[n]).wait()
            pltpu.make_async_remote_copy(
                src_ref=rows, dst_ref=rows, send_sem=fwd_send.at[kind], recv_sem=fwd_recv.at[n],
                device_id=(g_core, d), device_id_type=MESH).start()
        then()

        @pl.when(mine)
        def _():
            add_block(kind, own)
            rows = block_rows(kind, other)
            pltpu.make_async_copy(rows, rows, fwd_recv.at[n]).wait()
            add_block(kind, other)

    def side_of(kind, dd):
        return lax.rem(dd + kind, 2)

    def tile_copy(kind, n):
        slot = kind * CHIPS + my_tile
        return pltpu.make_async_remote_copy(
            src_ref=coded.at[kind, n], dst_ref=out.at[slot], send_sem=tile_send.at[kind], recv_sem=slot_recv.at[slot],
            device_id=(x * 2 + side_of(kind, d), c * HALF + n), device_id_type=MESH)

    def own_tile_copy(kind):
        return pltpu.make_async_copy(coded.at[kind, d - c * HALF], out.at[kind * CHIPS + my_tile], own_sem.at[kind])

    def stays(kind, dd):
        return jnp.logical_and(jnp.logical_and(dd == d, at_home), side_of(kind, d) == c)

    first = lax.rem(lax.div(d, many), 2)

    def encode(kind):
        def one(i, _):
            n = lax.rem(first + lax.div(i, many), 2) * many + lax.rem(d + i, many)
            total = sums[n]
            top = jnp.maximum(jnp.max(jnp.abs(total), axis=0, keepdims=True), 1e-30)
            e = jnp.ceil(jnp.log2(top))
            code = jnp.round(total * (STEPS / jnp.exp2(e)))
            coded[kind, n, 0:DB, :] = code.astype(jnp.int32).astype(jnp.int16)
            coded[kind, n, DB:CODE_ROWS, :] = jnp.broadcast_to(e, (8, LANES)).astype(jnp.int32).astype(jnp.int16)
            own = stays(kind, c * HALF + n)

            @pl.when(jnp.logical_not(own))
            def _():
                tile_copy(kind, n).start()

            @pl.when(own)
            def _():
                own_tile_copy(kind).start()
            return 0
        lax.fori_loop(0, HALF, one, 0)
        sums[...] = jnp.zeros_like(sums)

    def slot_copy(slot, send_sem, recv_sem, to_g):
        return pltpu.make_async_remote_copy(
            src_ref=out.at[slot], dst_ref=out.at[slot], send_sem=send_sem,
            recv_sem=recv_sem, device_id=(to_g, d), device_id_type=MESH)

    def arrived(slot):
        pltpu.make_async_copy(out.at[slot], out.at[slot], slot_recv.at[slot]).wait()

    def to_core(kind, slot):
        slot_copy(slot, core_send.at[0], core_recv.at[kind], g_core).start()

    def source(kind, j):
        i, m, b = lax.div(j, 4), lax.rem(lax.div(j, 2), 2), lax.rem(j, 2)
        k = 2 * m + lax.rem(d + c + kind, 2)
        return b * HALF + lax.rem(first + i, 2) * many + lax.rem(lax.rem(d, many) + many - k, many)

    def slot_at(kind, xx, dd):
        return kind * CHIPS + xx * PER_X + dd

    def from_dist(kind, j):
        dd = source(kind, j)
        slot = slot_at(kind, x, dd)

        @pl.when(dd < PER_X)
        def _():
            own = stays(kind, dd)

            @pl.when(own)
            def _():
                own_tile_copy(kind).wait()

            @pl.when(jnp.logical_not(own))
            def _():
                arrived(slot)
            slot_copy(slot, right_send.at[0], slot_recv.at[slot], g_right).start()
            slot_copy(slot, left_send.at[0], slot_recv.at[slot], g_left).start()
            to_core(kind, slot)

    def from_sides(kind, j):
        dd = source(kind, j)
        from_left = slot_at(kind, lax.rem(x + 3, 4), dd)
        from_right = slot_at(kind, lax.rem(x + 1, 4), dd)

        @pl.when(dd < PER_X)
        def _():
            arrived(from_left)

            @pl.when(lax.rem(lax.div(dd, 2), 2) == 0)
            def _():
                slot_copy(from_left, right_send.at[1], slot_recv.at[from_left], g_right).start()
            to_core(kind, from_left)
            arrived(from_right)

            @pl.when(lax.rem(lax.div(dd, 2), 2) == 1)
            def _():
                slot_copy(from_right, left_send.at[1], slot_recv.at[from_right], g_left).start()
            to_core(kind, from_right)

    def from_far(kind, j):
        dd = source(kind, j)

        @pl.when(dd < PER_X)
        def _():
            slot = slot_at(kind, lax.rem(x + 2, 4), dd)
            arrived(slot)
            to_core(kind, slot)

    def many_of(body, kind, start, stop):
        def one(j, _):
            body(kind, j)
            return 0
        lax.fori_loop(start, stop, one, 0)

    sums[...] = jnp.zeros_like(sums)
    for n in range(8):
        kind, r = n // 4, n % 4

        def then():
            if n + AHEAD < 8:
                rows_to((n + AHEAD) // 4, (n + AHEAD) % 4)
        phase(kind, r, then)
        if r == 3:
            @pl.when(mine)
            def _():
                encode(kind)
        if n == 5:
            many_of(from_dist, 0, 0, 4)
        if n == 6:
            many_of(from_dist, 0, 4, 8)
    many_of(from_sides, 0, 0, 8)
    many_of(from_dist, 1, 0, 4)
    many_of(from_far, 0, 0, 8)
    many_of(from_dist, 1, 4, 8)

    def wait_slots(sem, n):
        ref = out.at[pl.ds(0, n)]
        pltpu.make_async_copy(ref, ref, sem).wait()

    def from_core(kind):
        @pl.when(c == 1 - kind)
        def _():
            wait_slots(core_recv.at[kind], 4 * 8)

        @pl.when(c == kind)
        def _():
            wait_slots(core_recv.at[kind], 4 * 7)
    from_core(0)

    def load_tile(t, _):
        loading[pl.ds(pl.multiple_of(t * SPREAD, 8), DB), :] = decode(out, t)
        return 0
    lax.fori_loop(0, TABLE_TILES, load_tile, 0)
    paired[...] = jnp.zeros_like(paired)
    low_row = lax.broadcasted_iota(jnp.int32, (TABLE_TILES, LANES), 1) < RANK
    low_full = lax.broadcasted_iota(jnp.int32, (LANES, LANES), 1) < RANK

    def group(grp, _):
        for k in range(GROUP):
            rows = loading[pl.ds(grp * GROUP + k, TABLE_TILES, stride=SPREAD), :]
            turned = pltpu.roll(rows, RANK, axis=1)
            paired[k, pl.ds(0, TABLE_TILES, stride=2), :] = jnp.where(low_row, rows, turned)
            paired[k, pl.ds(1, TABLE_TILES, stride=2), :] = jnp.where(low_row, turned, rows)
        for k in range(GROUP):
            full = paired[k]
            hi = full.astype(jnp.bfloat16)
            lo = (full - hi.astype(jnp.float32)).astype(jnp.bfloat16)
            mixed = jnp.where(low_full, hi, lo)
            left = jnp.concatenate([mixed, mixed], axis=1)
            right = jnp.concatenate([hi, lo], axis=1)
            product = lax.dot_general(left, right, (((1,), (1,)), ((), ())), preferred_element_type=jnp.float32)
            outer[pl.ds(pl.multiple_of((grp * GROUP + k) * CROWS, 8), CROWS), :] = product[0:CROWS, :]

        @pl.when(grp < 8)
        def _():
            from_sides(1, grp)

        @pl.when(grp >= 8)
        def _():
            from_far(1, grp - 8)
        return 0
    lax.fori_loop(0, DB // GROUP, group, 0)

    from_core(1)
    wait_slots(core_send.at[0], 4 * PER_X)
    wait_slots(right_send.at[0], PER_X)
    wait_slots(left_send.at[0], PER_X)
    wait_slots(right_send.at[1], 8)
    wait_slots(left_send.at[1], 7)

    @pl.when(at_home)
    def _():
        pk_wait(DIST - 1, pk_send)

    for kind in range(2):
        def wait_rows(sem, n):
            ref = table.at[kind, pl.ds(0, n), :]
            pltpu.make_async_copy(ref, ref, sem.at[kind]).wait()

        @pl.when(mine)
        def _():
            wait_rows(row_send, (CHIPS - 1) * ROWS)
            wait_rows(fwd_send, 4 * BLOCK)
            own = stays(kind, d)

            @pl.when(own)
            def _():
                wait_slots(tile_send.at[kind], HALF - 1)

            @pl.when(jnp.logical_not(own))
            def _():
                wait_slots(tile_send.at[kind], HALF)

        @pl.when(jnp.logical_not(mine))
        def _():
            wait_rows(row_send, CHIPS * ROWS)


def tile_sums(idx, wgt, est, fac, var):
    vmem = pl.BlockSpec(memory_space=pltpu.VMEM)
    hbm = pl.BlockSpec(memory_space=pltpu.MemorySpace.HBM)
    dma = pltpu.SemaphoreType.DMA
    return pl.pallas_call(
        sums_kernel,
        out_shape=(jax.ShapeDtypeStruct((SLOTS, CODE_ROWS, LANES), jnp.int16),
                   jax.ShapeDtypeStruct((DB * CROWS, LANES), jnp.float32)),
        in_specs=[hbm] * 5,
        out_specs=(vmem, vmem),
        scratch_shapes=[
            pltpu.VMEM((INTER, DB), jnp.int32),
            pltpu.VMEM((INTER, DB), jnp.int32),
            pltpu.VMEM(est.shape, jnp.bfloat16),
            pltpu.VMEM(fac.shape, jnp.bfloat16),
            pltpu.VMEM(var.shape, jnp.bfloat16),
            dma((5,)),
            pltpu.VMEM((DIST, INTER, DB), jnp.int32),
            pltpu.VMEM((ROWS, LANES), jnp.bfloat16),
            pltpu.VMEM((2, TRACTS, LANES), jnp.bfloat16),
            pltpu.VMEM((HALF, DB, LANES), jnp.bfloat16),
            pltpu.VMEM((HALF, DB, LANES), jnp.bfloat16),
            pltpu.VMEM((HALF, DB, LANES), jnp.float32),
            pltpu.VMEM((2, HALF, CODE_ROWS, LANES), jnp.int16),
            pltpu.SemaphoreType.REGULAR, dma((2,)), dma((1,)), dma((1,)), dma((2,)), dma((8,)), dma((2,)), dma((8,)),
            dma((2,)), dma((SLOTS,)), dma((2,)), dma((2,)), dma((1,)), dma((2,)),
            pltpu.VMEM(((TABLE_TILES + 6) * SPREAD, LANES), jnp.float32),
            pltpu.VMEM((GROUP, LANES, LANES), jnp.float32),
        ],
        compiler_params=pltpu.CompilerParams(has_side_effects=True, collective_id=0, vmem_limit_bytes=32 * 2**20),
        name="tile_sums",
    )(idx, wgt, est, fac, var)


CHUNK = 4


def blocks_kernel(slots, outer, marg_hbm, cov_hbm, marg, noise, flat, marg_sem, cov_sem):
    noise[...] = jnp.transpose(decode(slots, HI) + decode(slots, LO) * (1.0 / 256.0))
    sub = lax.broadcasted_iota(jnp.int32, (LANES, LANES), 0)

    span = CHUNK * AGES

    def cov_copy(n):
        rows = pl.ds(pl.multiple_of(n * span, 8), span)
        return pltpu.make_async_copy(flat.at[rows, :], cov_hbm.at[rows, :], cov_sem)

    def ages(n, _):
        for pair in range(CHUNK // 2):
            halves = []
            for h in range(2):
                i = n * CHUNK + pair * 2 + h
                block = jnp.transpose(outer[pl.ds(i, DB, stride=CROWS), :])
                block = block + jnp.where(sub == i, noise[pl.ds(i, 1), :], 0.0)
                halves.append(block[0:AGES, :])
            flat[pl.ds(pl.multiple_of(n * span + pair * 2 * AGES, 8), 2 * AGES), :] = jnp.concatenate(halves, axis=0)
        cov_copy(n).start()
        return 0
    lax.fori_loop(0, AGES // CHUNK, ages, 0)
    for t in range(TABLE_TILES):
        marg[:, t * LANES:(t + 1) * LANES] = decode(slots, CHIPS + t)
    out_marg = pltpu.make_async_copy(marg, marg_hbm, marg_sem)
    out_marg.start()
    pltpu.make_async_copy(flat, cov_hbm, cov_sem).wait()
    out_marg.wait()


def blocks(slots, outer):
    vmem = pl.BlockSpec(memory_space=pltpu.VMEM)
    hbm = pl.BlockSpec(memory_space=pltpu.MemorySpace.HBM)
    dma = pltpu.SemaphoreType.DMA
    marg, cov = pl.pallas_call(
        blocks_kernel,
        out_shape=(jax.ShapeDtypeStruct((DB, TABLE_TILES * LANES), jnp.float32),
                   jax.ShapeDtypeStruct((AGES * AGES, DB), jnp.float32)),
        in_specs=[vmem, vmem],
        out_specs=(hbm, hbm),
        scratch_shapes=[
            pltpu.VMEM((DB, TABLE_TILES * LANES), jnp.float32),
            pltpu.VMEM((DB, LANES), jnp.float32),
            pltpu.VMEM((AGES * AGES, DB), jnp.float32),
            dma(()), dma(()),
        ],
        compiler_params=pltpu.CompilerParams(vmem_limit_bytes=24 * 2**20),
        name="district_blocks",
    )(slots, outer)
    return marg, cov.T


def shards(estimates, factors, variances, intersection_tracts, intersection_weights):
    keep = lambda a: pltpu.with_memory_space_constraint(a, pltpu.MemorySpace.HBM)
    slots, outer = tile_sums(keep(intersection_tracts.T), keep(intersection_weights.T), keep(estimates), keep(factors), keep(variances))
    return blocks(slots, outer)


def solution(mesh):
    return jax.shard_map(
        shards,
        mesh=mesh,
        in_specs=(
            P(("geo", "dist"), None),
            P(("geo", "dist"), None),
            P(("geo", "dist"), None),
            P("dist", None),
            P("dist", None),
        ),
        out_specs=(P("dist", None), P("dist", None)),
        check_vma=False,
    )
```
